512 devices in a mesh: dp: 16 (over z), shard: 32 (over y, x, core).
Axes of the slice: x: 4, y: 4, z: 16, core: 2. Of those that a mesh axis runs over, the one named last changes fastest.
Arguments:
- hidden_in: bfloat16 [16384, 5120], P('dp', 'shard'), may hold values from -6 to 6
- context_in: bfloat16 [16384, 5120], P('dp', 'shard'), may hold values from -6 to 6
- query_cotan: bfloat16 [16384, 2560], P('dp', 'shard'), may hold values from -0.1875 to 0.1875
- output_cotan: bfloat16 [16384, 2560], P('dp', 'shard'), may hold values from -0.1875 to 0.1875
- query_error: bfloat16 [16, 5120, 2560], P('dp', 'shard'), may hold values from -3 to 3
- output_error: bfloat16 [16, 5120, 2560], P('dp', 'shard'), may hold values from -3 to 3
- query_weight: float32 [5120, 2560], P('shard', 'dp'), may hold values from -0.6 to 0.6
- output_weight: float32 [5120, 2560], P('shard', 'dp'), may hold values from -0.6 to 0.6
- start_factors: bfloat16 [2, 2560, 32], replicated, may hold values from -0.09863281 to 0.09863281
Outputs:
- query_error_new: bfloat16 [16, 5120, 2560], P('dp', 'shard')
- output_error_new: bfloat16 [16, 5120, 2560], P('dp', 'shard')
- query_weight_new: float32 [5120, 2560], P('shard', 'dp')
- output_weight_new: float32 [5120, 2560], P('shard', 'dp')
The draws below stay inside these ranges and needn't reach their ends.
All inputs are finite; a program needn't handle non-finite values.
Results may differ from the reference program's by a relative error of at most 0.005.
Values may be sent and summed in bfloat16 or wider, within the bound.
No kernel may reach another device: no remote copies, remote signals or barrier semaphores. Data moves between devices by JAX's collectives and lax.ppermute only.
A program may use at most 64 MiB of HBM per device.

```python
import jax
import jax.numpy as jnp
from jax import lax

D = 5120
DOUT = 2560
RANK = 32
TOK = 1024
TOKENS = 16384
N_DP = 16


def block_scale(stream_key, dims, split, smallest, top_value):
    def one(position, shards_of):
        heights = jax.random.uniform(jax.random.fold_in(jax.random.fold_in(stream_key, 6), position), (shards_of,), jnp.float32, smallest / len(split), top_value / len(split))
        return jnp.repeat(jnp.exp(heights), dims[position] // shards_of).reshape((-1,) + (1,) * (len(dims) - position - 1))

    gain = one(*split[0])
    for cut in split[1:]:
        gain = gain * one(*cut)
    return gain


def scatter_about(rng, extent, width, limit, cuts=(), held_as=jnp.bfloat16):
    entries = width * jax.random.normal(rng, extent, jnp.float32)
    if cuts:
        entries = entries * block_scale(rng, extent, cuts, -0.22, 0.18)
    return jnp.clip(entries, -limit, limit).astype(held_as)


def setup_inputs(seed: int = 0) -> dict:
    key_list = jax.random.split(jax.random.key(seed), 10)
    hidden_in = scatter_about(key_list[0], (TOKENS, D), 1.0, 6.0, ((0, 16), (1, 32)))
    context_in = scatter_about(key_list[1], (TOKENS, D), 1.0, 6.0, ((0, 16), (1, 32)))
    query_cotan = scatter_about(key_list[2], (TOKENS, DOUT), (TOK ** -0.5), 0.1875, ((0, 16), (1, 32)))
    output_cotan = scatter_about(key_list[3], (TOKENS, DOUT), (TOK ** -0.5), 0.1875, ((0, 16), (1, 32)))
    query_error = scatter_about(key_list[4], (N_DP, D, DOUT), 0.5, 3.0, ((0, 16), (1, 32)))
    output_error = scatter_about(key_list[5], (N_DP, D, DOUT), 0.5, 3.0, ((0, 16), (1, 32)))
    query_weight = scatter_about(key_list[6], (D, DOUT), 0.1, 0.6, ((0, 32), (1, 16)), jnp.float32)
    output_weight = scatter_about(key_list[7], (D, DOUT), 0.1, 0.6, ((0, 32), (1, 16)), jnp.float32)
    start_factors = scatter_about(key_list[8], (2, DOUT, RANK), (DOUT ** -0.5), 0.09863281)
    return {"hidden_in": hidden_in, "context_in": context_in, "query_cotan": query_cotan, "output_cotan": output_cotan, "query_error": query_error, "output_error": output_error, "query_weight": query_weight, "output_weight": output_weight, "start_factors": start_factors}


HIGH = lax.Precision.HIGHEST

def compress(inputs, cotan, error, weight, start):
    acts = inputs.reshape(N_DP, TOK, D)
    grads = cotan.reshape(N_DP, TOK, DOUT)
    start32 = start.astype(jnp.float32)

    def form(index):
        grad = lax.dot_general(acts[index].astype(jnp.float32), grads[index].astype(jnp.float32), (((0,), (0,)), ((), ())), preferred_element_type=jnp.float32)
        return grad + error[index].astype(jnp.float32)
    full = lax.map(form, jnp.arange(N_DP, dtype=jnp.int32))
    left = jnp.einsum('rdo,ok->dk', full, start32, precision=HIGH) / jnp.float32(N_DP)
    gram = jnp.dot(left.T, left, precision=HIGH)
    chol = jnp.linalg.cholesky(gram)
    ortho = lax.linalg.triangular_solve(chol, left, left_side=False, lower=True, transpose_a=True)
    right = jnp.einsum('rdo,dk->ok', full, ortho, precision=HIGH) / jnp.float32(N_DP)
    approx = jnp.dot(ortho, right.T, precision=HIGH)
    error_new = (full - approx[None]).astype(jnp.bfloat16)
    return (error_new, weight - approx)

def reference(hidden_in, context_in, query_cotan, output_cotan, query_error, output_error, query_weight, output_weight, start_factors):
    query_error_new, query_weight_new = compress(hidden_in, query_cotan, query_error, query_weight, start_factors[0])
    output_error_new, output_weight_new = compress(context_in, output_cotan, output_error, output_weight, start_factors[1])
    return (query_error_new, output_error_new, query_weight_new, output_weight_new)
```

```python
import jax
import jax.numpy as jnp
from jax import lax
from jax.sharding import PartitionSpec as P

HIGH = lax.Precision.HIGHEST
F32 = jnp.float32
BF16 = jnp.bfloat16


def copies(array, count):
    return jnp.broadcast_to(array, (count, *array.shape))


def exchange(array, axis, groups=None):
    return lax.all_to_all(array, axis, 0, 0, tiled=True, axis_index_groups=groups)


def from_everyone(array, axis):
    return exchange(copies(array, lax.axis_size(axis)), axis)


def split_high_low(array):
    high = array.astype(BF16)
    return high, (array - high.astype(F32)).astype(BF16)


def side_by_side(query, output):
    half = query.shape[-2] // 2
    return jnp.concatenate(
        [query[..., :half, :], output[..., :half, :], query[..., half:, :], output[..., half:, :]],
        axis=-1,
    )


def apart(both):
    rank = both.shape[-1] // 4
    parts = [both[..., i * rank : (i + 1) * rank] for i in range(4)]
    return (
        jnp.concatenate([parts[0], parts[2]], axis=-2),
        jnp.concatenate([parts[1], parts[3]], axis=-2),
    )


def all_columns(cotan):
    shards = lax.axis_size("shard")
    chips = shards // 2
    same_core = [[2 * chip + core for chip in range(chips)] for core in range(2)]
    swap = [(i, i ^ 1) for i in range(shards)]
    mine = exchange(copies(cotan.T, chips), "shard", same_core)
    theirs = lax.ppermute(mine, "shard", swap)
    first = lax.axis_index("shard") % 2 == 0
    both = jnp.stack(
        [jnp.where(first, mine, theirs), jnp.where(first, theirs, mine)], axis=1
    )
    return both.reshape(-1, cotan.shape[0])


def contract(a, b, dims):
    return lax.dot_general(a, b, ((dims[:1], dims[1:]), ((), ())), preferred_element_type=F32)


def full_gradient(inputs, columns, error):
    return contract(inputs.T, columns, (1, 1)) + error[0].astype(F32)


def inverse_factor(gram):
    chol = jnp.linalg.cholesky(gram)
    eye = jnp.eye(gram.shape[0], dtype=F32)
    return lax.linalg.triangular_solve(chol, eye, left_side=True, lower=True)


def body(
    hidden_in,
    context_in,
    query_cotan,
    output_cotan,
    query_error,
    output_error,
    query_weight,
    output_weight,
    start_factors,
):
    replicas = lax.axis_size("dp")
    shards = lax.axis_size("shard")
    start = start_factors.astype(F32)

    query_full = full_gradient(hidden_in, all_columns(query_cotan), query_error)
    output_full = full_gradient(context_in, all_columns(output_cotan), output_error)
    query_left = jnp.dot(query_full, start[0], precision=HIGH)
    output_left = jnp.dot(output_full, start[1], precision=HIGH)

    lefts = from_everyone(side_by_side(query_left, output_left).astype(BF16), "dp")
    query_left, output_left = apart(lefts.astype(F32).sum(axis=0) / F32(replicas))

    def term(full, left):
        product = lax.dot_general(full, left, (((0,), (0,)), ((), ())), precision=HIGH)
        return product.reshape(shards, -1, product.shape[-1])

    def gram_of(left):
        return lax.dot_general(left, left, (((0,), (0,)), ((), ())), precision=HIGH)

    terms = side_by_side(term(query_full, query_left), term(output_full, output_left))
    rows = terms.shape[1]
    grams = jnp.concatenate(
        [*split_high_low(gram_of(query_left)), *split_high_low(gram_of(output_left))], axis=1
    )
    rank = grams.shape[0]
    sent = jnp.concatenate([terms.astype(BF16), copies(grams, shards)], axis=1)
    arrived = exchange(sent, "shard").astype(F32).sum(axis=0)
    share = arrived[:rows]
    gram_parts = arrived[rows:]

    shares = from_everyone(share.astype(BF16), "dp")
    share = shares.astype(F32).sum(axis=0) / F32(replicas)

    query_inverse = inverse_factor(gram_parts[:, :rank] + gram_parts[:, rank : 2 * rank])
    output_inverse = inverse_factor(gram_parts[:, 2 * rank : 3 * rank] + gram_parts[:, 3 * rank :])

    def weighted(left, inverse):
        ortho = lax.dot_general(left, inverse, (((1,), (1,)), ((), ())), precision=HIGH)
        high, low = split_high_low(jnp.dot(ortho, inverse, precision=HIGH))
        return jnp.concatenate([high, low], axis=1)

    query_rows = weighted(query_left, query_inverse)
    output_rows = weighted(output_left, output_inverse)

    query_cols, output_cols = apart(from_everyone(share.astype(BF16), "shard"))

    def finish(rows, cols, full, weight):
        cols = cols.reshape(-1, cols.shape[-1])
        cols = jnp.concatenate([cols, cols], axis=1)
        width = weight.shape[1]
        own = lax.dynamic_slice_in_dim(cols, lax.axis_index("dp") * width, width, 0)
        error_new = (full - contract(rows, cols, (1, 1))).astype(BF16)[None]
        return error_new, weight - contract(rows, own, (1, 1))

    query_error_new, query_weight_new = finish(query_rows, query_cols, query_full, query_weight)
    output_error_new, output_weight_new = finish(
        output_rows, output_cols, output_full, output_weight
    )
    return query_error_new, output_error_new, query_weight_new, output_weight_new


def solution(mesh):
    placed = (
        P("dp", "shard"),
        P("dp", "shard"),
        P("dp", "shard"),
        P("dp", "shard"),
        P("dp", "shard", None),
        P("dp", "shard", None),
        P("shard", "dp"),
        P("shard", "dp"),
        P(),
    )
    return jax.shard_map(
        body,
        mesh=mesh,
        in_specs=placed,
        out_specs=(
            P("dp", "shard", None),
            P("dp", "shard", None),
            P("shard", "dp"),
            P("shard", "dp"),
        ),
        check_vma=False,
    )
```

```python
import jax
import jax.numpy as jnp
from jax import lax
from jax.sharding import PartitionSpec as P


HIGH = lax.Precision.HIGHEST
F32 = jnp.float32
BF16 = jnp.bfloat16


def copies(array, count):
    return jnp.broadcast_to(array, (count, *array.shape))


def exchange(array, axis, groups=None):
    return lax.all_to_all(array, axis, 0, 0, tiled=True, axis_index_groups=groups)


def from_everyone(array, axis):
    return exchange(copies(array, lax.axis_size(axis)), axis)


def split_high_low(array):
    high = array.astype(BF16)
    return high, (array - high.astype(F32)).astype(BF16)


def side_by_side(query, output):
    half = query.shape[-2] // 2
    return jnp.concatenate(
        [query[..., :half, :], output[..., :half, :], query[..., half:, :], output[..., half:, :]],
        axis=-1,
    )


def apart(both):
    rank = both.shape[-1] // 4
    parts = [both[..., i * rank : (i + 1) * rank] for i in range(4)]
    return (
        jnp.concatenate([parts[0], parts[2]], axis=-2),
        jnp.concatenate([parts[1], parts[3]], axis=-2),
    )


def in_plane(rows, cols, core):
    side = 4
    pairs = []
    for y in range(side):
        for x in range(side):
            for c in range(2):
                to = ((y + rows) % side * side + (x + cols) % side) * 2 + (c + core) % 2
                pairs.append(((y * side + x) * 2 + c, to))
    return pairs


def send(array, rows, cols, core=0):
    return lax.ppermute(array, "shard", in_plane(rows, cols, core))


def in_order(pieces, position):
    count = len(pieces)
    result = jnp.zeros((count, *pieces[0].shape), pieces[0].dtype)
    for k, piece in enumerate(pieces):
        at = (position + k) % count
        result = lax.dynamic_update_slice_in_dim(result, piece[None], at, 0)
    return result


def by_exchange(cotan):
    chips = lax.axis_size("shard") // 2
    same_core = [[2 * chip + core for chip in range(chips)] for core in range(2)]
    return exchange(copies(cotan.T, chips), "shard", same_core)


def by_rings(cotan):
    shard = lax.axis_index("shard")
    y, x = shard // 8, shard // 2 % 4
    block = cotan.T
    below, above, across = send(block, 1, 0), send(block, 3, 0), send(block, 2, 0)
    column = in_order([block, above, across, below], y)
    left, right = send(column, 0, 1), send(column, 0, 3)
    half = column.shape[0] // 2
    far = jnp.concatenate([send(left[:half], 0, 1), send(right[half:], 0, 3)])
    return jnp.swapaxes(in_order([column, right, far, left], x), 0, 1)


def all_columns(mine):
    theirs = send(mine, 0, 0, 1)
    tokens = mine.shape[-1]
    core = lax.axis_index("shard") % 2
    both = jnp.zeros((mine.size // mine.shape[-2] // tokens, 2, *mine.shape[-2:]), mine.dtype)
    for array, at in ((mine, core), (theirs, 1 - core)):
        array = array.reshape(-1, 1, *mine.shape[-2:])
        both = lax.dynamic_update_slice_in_dim(both, array, at, 1)
    return both.reshape(-1, tokens)


def contract(a, b, dims):
    return lax.dot_general(a, b, ((dims[:1], dims[1:]), ((), ())), preferred_element_type=F32)


def full_gradient(inputs, columns, error):
    return contract(inputs.T, columns, (1, 1)) + error[0].astype(F32)


def inverse_factor(gram):
    chol = jnp.linalg.cholesky(gram)
    eye = jnp.eye(gram.shape[0], dtype=F32)
    return lax.linalg.triangular_solve(chol, eye, left_side=True, lower=True)


def step(
    hidden_in,
    context_in,
    query_cotan,
    output_cotan,
    query_error,
    output_error,
    query_weight,
    output_weight,
    start_factors,
):
    replicas = lax.axis_size("dp")
    shards = lax.axis_size("shard")
    start = start_factors.astype(F32)

    query_blocks = by_exchange(query_cotan)
    query_columns = all_columns(query_blocks)
    output_columns = all_columns(by_rings(output_cotan))
    query_full = full_gradient(hidden_in, query_columns, query_error)
    output_full = full_gradient(context_in, output_columns, output_error)
    query_left = jnp.dot(query_full, start[0], precision=HIGH)
    output_left = jnp.dot(output_full, start[1], precision=HIGH)

    lefts = from_everyone(side_by_side(query_left, output_left).astype(BF16), "dp")
    query_left, output_left = apart(lefts.astype(F32).sum(axis=0) / F32(replicas))

    def term(full, left):
        product = lax.dot_general(full, left, (((0,), (0,)), ((), ())), precision=HIGH)
        return product.reshape(shards, -1, product.shape[-1])

    def gram_of(left):
        return lax.dot_general(left, left, (((0,), (0,)), ((), ())), precision=HIGH)

    terms = side_by_side(term(query_full, query_left), term(output_full, output_left))
    rows = terms.shape[1]
    grams = jnp.concatenate(
        [*split_high_low(gram_of(query_left)), *split_high_low(gram_of(output_left))], axis=1
    )
    rank = grams.shape[0]
    sent = jnp.concatenate([terms.astype(BF16), copies(grams, shards)], axis=1)
    arrived = exchange(sent, "shard").astype(F32).sum(axis=0)
    share = arrived[:rows]
    gram_parts = arrived[rows:]

    shares = from_everyone(share.astype(BF16), "dp")
    share = shares.astype(F32).sum(axis=0) / F32(replicas)

    query_inverse = inverse_factor(gram_parts[:, :rank] + gram_parts[:, rank : 2 * rank])
    output_inverse = inverse_factor(gram_parts[:, 2 * rank : 3 * rank] + gram_parts[:, 3 * rank :])

    def weighted(left, inverse):
        ortho = lax.dot_general(left, inverse, (((1,), (1,)), ((), ())), precision=HIGH)
        high, low = split_high_low(jnp.dot(ortho, inverse, precision=HIGH))
        return jnp.concatenate([high, low], axis=1)

    query_rows = weighted(query_left, query_inverse)
    output_rows = weighted(output_left, output_inverse)

    query_cols, output_cols = apart(from_everyone(share.astype(BF16), "shard"))

    def finish(rows, cols, full, weight):
        cols = cols.reshape(-1, cols.shape[-1])
        cols = jnp.concatenate([cols, cols], axis=1)
        width = weight.shape[1]
        own = lax.dynamic_slice_in_dim(cols, lax.axis_index("dp") * width, width, 0)
        error_new = (full - contract(rows, cols, (1, 1))).astype(BF16)[None]
        return error_new, weight - contract(rows, own, (1, 1))

    query_error_new, query_weight_new = finish(query_rows, query_cols, query_full, query_weight)
    output_error_new, output_weight_new = finish(
        output_rows, output_cols, output_full, output_weight
    )
    return query_error_new, output_error_new, query_weight_new, output_weight_new


def solution(mesh):
    placed = (
        P("dp", "shard"),
        P("dp", "shard"),
        P("dp", "shard"),
        P("dp", "shard"),
        P("dp", "shard", None),
        P("dp", "shard", None),
        P("shard", "dp"),
        P("shard", "dp"),
        P(),
    )
    return jax.shard_map(
        step,
        mesh=mesh,
        in_specs=placed,
        out_specs=(
            P("dp", "shard", None),
            P("dp", "shard", None),
            P("shard", "dp"),
            P("shard", "dp"),
        ),
        check_vma=False,
    )
```

```python
import functools

import jax
import jax.numpy as jnp
from jax import lax
from jax.experimental import pallas as pl
from jax.experimental.pallas import tpu as pltpu
from jax.sharding import PartitionSpec as P


HIGH = lax.Precision.HIGHEST
F32 = jnp.float32
BF16 = jnp.bfloat16


def copies(array, count):
    return jnp.broadcast_to(array, (count, *array.shape))


def exchange(array, axis, groups=None):
    return lax.all_to_all(array, axis, 0, 0, tiled=True, axis_index_groups=groups)


def from_everyone(array, axis):
    return exchange(copies(array, lax.axis_size(axis)), axis)


def split_high_low(array):
    high = array.astype(BF16)
    return high, (array - high.astype(F32)).astype(BF16)


def side_by_side(query, output):
    half = query.shape[-2] // 2
    return jnp.concatenate(
        [query[..., :half, :], output[..., :half, :], query[..., half:, :], output[..., half:, :]],
        axis=-1,
    )


def apart(both):
    rank = both.shape[-1] // 4
    parts = [both[..., i * rank : (i + 1) * rank] for i in range(4)]
    return (
        jnp.concatenate([parts[0], parts[2]], axis=-2),
        jnp.concatenate([parts[1], parts[3]], axis=-2),
    )


def in_plane(rows, cols, core):
    side = 4
    pairs = []
    for y in range(side):
        for x in range(side):
            for c in range(2):
                to = ((y + rows) % side * side + (x + cols) % side) * 2 + (c + core) % 2
                pairs.append(((y * side + x) * 2 + c, to))
    return pairs


def send(array, rows, cols, core=0):
    return lax.ppermute(array, "shard", in_plane(rows, cols, core))


def by_exchange(cotan):
    side = 4
    rows = [[(y * side + x) * 2 + c for x in range(side)] for y in range(side) for c in range(2)]
    cols = [[(y * side + x) * 2 + c for y in range(side)] for x in range(side) for c in range(2)]
    row = exchange(copies(cotan.T, side), "shard", rows)
    return exchange(copies(row, side), "shard", cols)


def by_rings(cotan):
    block = cotan.T
    below, above, across = send(block, 1, 0), send(block, 3, 0), send(block, 2, 0)
    column = jnp.stack([block, above, across, below])
    left, right = send(column, 0, 1), send(column, 0, 3)
    half = column.shape[0] // 2
    far = jnp.concatenate([send(left[:half], 0, 1), send(right[half:], 0, 3)])
    return column, right, far, left


def partner(array):
    return send(array, 0, 0, 1)


def gradient_kernel(blocks, place, acts, error, start, *refs):
    sources, (full, left, columns, done) = refs[:-4], refs[-4:]
    mine, theirs = sources[: len(sources) // 2], sources[len(sources) // 2 :]
    side, each = 4, columns.shape[1] // 8
    y0, x0, core = place[0], place[1], place[2]

    def fetch(j, k, other):
        source = blocks(theirs if other else mine, j, k)
        at = ((x0 + k) % side * 2 + (1 - core if other else core)) * each
        return pltpu.make_async_copy(
            source,
            columns.at[j, pl.ds(pl.multiple_of(at, 16), each), :],
            done.at[j, k * 2 + other],
        )

    steps = [(k, other) for k in range(side) for other in range(2)]
    for j in range(side):
        for k, other in steps:
            fetch(j, k, other).start()
    total = jnp.zeros(left.shape, F32)
    for j in range(side):
        for k, other in steps:
            fetch(j, k, other).wait()
        here = pl.ds(pl.multiple_of((y0 + j) % side * (8 * each), 128), 8 * each)
        part = contract(acts[...], columns[j], (1, 1)) + error[:, here].astype(F32)
        full[:, here] = part
        high, low = split_high_low(part)
        factor = start[:, here]
        total += contract(high, factor, (1, 1)) + contract(low, factor, (1, 1))
    left[...] = total


def full_gradient(inputs, error, start, mine, theirs, blocks, place):
    rows, tokens = inputs.shape[::-1]
    width, rank = error.shape[-1], start.shape[-1]
    vmem = pl.BlockSpec(memory_space=pltpu.VMEM)
    return pl.pallas_call(
        functools.partial(gradient_kernel, blocks),
        out_shape=(
            jax.ShapeDtypeStruct((rows, width), F32),
            jax.ShapeDtypeStruct((rows, rank), F32),
        ),
        in_specs=[
            pl.BlockSpec(memory_space=pltpu.SMEM),
            vmem,
            vmem,
            vmem,
            *[pl.BlockSpec(memory_space=pl.ANY)] * (len(mine) + len(theirs)),
        ],
        out_specs=(vmem, vmem),
        scratch_shapes=[
            pltpu.VMEM((4, width // 4, tokens), BF16),
            pltpu.SemaphoreType.DMA((4, 8)),
        ],
    )(place, inputs.T, error[0], start.T, *mine, *theirs)


def contract(a, b, dims):
    return lax.dot_general(a, b, ((dims[:1], dims[1:]), ((), ())), preferred_element_type=F32)


def inverse_factor(gram):
    chol = jnp.linalg.cholesky(gram)
    eye = jnp.eye(gram.shape[0], dtype=F32)
    return lax.linalg.triangular_solve(chol, eye, left_side=True, lower=True)


def step(
    hidden_in,
    context_in,
    query_cotan,
    output_cotan,
    query_error,
    output_error,
    query_weight,
    output_weight,
    start_factors,
):
    replicas = lax.axis_size("dp")
    shards = lax.axis_size("shard")
    shard = lax.axis_index("shard")
    y, x, core = shard // 8, shard // 2 % 4, shard % 2
    query_mine = (by_exchange(query_cotan),)
    query_theirs = [partner(a) for a in query_mine]
    output_mine = by_rings(output_cotan)
    query_full, query_left = full_gradient(
        hidden_in,
        query_error,
        start_factors[0],
        query_mine,
        query_theirs,
        lambda refs, j, k: refs[0].at[j, k],
        jnp.stack([0 * core, 0 * core, core]),
    )
    column, right, far, left = output_mine
    far = partner(far)
    output_full, output_left = full_gradient(
        context_in,
        output_error,
        start_factors[1],
        output_mine,
        [partner(column), partner(right), far, partner(left)],
        lambda refs, j, k: refs[k].at[j],
        jnp.stack([y, x, core]),
    )

    lefts = from_everyone(side_by_side(query_left, output_left).astype(BF16), "dp")
    query_left, output_left = apart(lefts.astype(F32).sum(axis=0) / F32(replicas))

    def term(full, left):
        product = lax.dot_general(full, left, (((0,), (0,)), ((), ())), precision=HIGH)
        return product.reshape(shards, -1, product.shape[-1])

    def gram_of(left):
        return lax.dot_general(left, left, (((0,), (0,)), ((), ())), precision=HIGH)

    terms = side_by_side(term(query_full, query_left), term(output_full, output_left))
    rows = terms.shape[1]
    grams = jnp.concatenate(
        [*split_high_low(gram_of(query_left)), *split_high_low(gram_of(output_left))], axis=1
    )
    rank = grams.shape[0]
    sent = jnp.concatenate([terms.astype(BF16), copies(grams, shards)], axis=1)
    arrived = exchange(sent, "shard").astype(F32).sum(axis=0)
    share = arrived[:rows]
    gram_parts = arrived[rows:]

    shares = from_everyone(share.astype(BF16), "dp")
    share = shares.astype(F32).sum(axis=0) / F32(replicas)

    query_inverse = inverse_factor(gram_parts[:, :rank] + gram_parts[:, rank : 2 * rank])
    output_inverse = inverse_factor(gram_parts[:, 2 * rank : 3 * rank] + gram_parts[:, 3 * rank :])

    def weighted(left, inverse):
        ortho = lax.dot_general(left, inverse, (((1,), (1,)), ((), ())), precision=HIGH)
        high, low = split_high_low(jnp.dot(ortho, inverse, precision=HIGH))
        return jnp.concatenate([high, low], axis=1)

    query_rows = weighted(query_left, query_inverse)
    output_rows = weighted(output_left, output_inverse)

    query_cols, output_cols = apart(from_everyone(share.astype(BF16), "shard"))

    def finish(rows, cols, full, weight):
        cols = cols.reshape(-1, cols.shape[-1])
        cols = jnp.concatenate([cols, cols], axis=1)
        width = weight.shape[1]
        own = lax.dynamic_slice_in_dim(cols, lax.axis_index("dp") * width, width, 0)
        error_new = (full - contract(rows, cols, (1, 1))).astype(BF16)[None]
        return error_new, weight - contract(rows, own, (1, 1))

    query_error_new, query_weight_new = finish(query_rows, query_cols, query_full, query_weight)
    output_error_new, output_weight_new = finish(
        output_rows, output_cols, output_full, output_weight
    )
    return query_error_new, output_error_new, query_weight_new, output_weight_new


def solution(mesh):
    placed = (
        P("dp", "shard"),
        P("dp", "shard"),
        P("dp", "shard"),
        P("dp", "shard"),
        P("dp", "shard", None),
        P("dp", "shard", None),
        P("shard", "dp"),
        P("shard", "dp"),
        P(),
    )
    return jax.shard_map(
        step,
        mesh=mesh,
        in_specs=placed,
        out_specs=(
            P("dp", "shard", None),
            P("dp", "shard", None),
            P("shard", "dp"),
            P("shard", "dp"),
        ),
        check_vma=False,
    )
```

```python
import functools

import jax
import jax.numpy as jnp
from jax import lax
from jax.experimental import pallas as pl
from jax.experimental.pallas import tpu as pltpu
from jax.sharding import PartitionSpec as P


HIGH = lax.Precision.HIGHEST
F32 = jnp.float32
BF16 = jnp.bfloat16


def copies(array, count):
    return jnp.broadcast_to(array, (count, *array.shape))


def exchange(array, axis, groups=None):
    return lax.all_to_all(array, axis, 0, 0, tiled=True, axis_index_groups=groups)


def from_everyone(array, axis):
    return exchange(copies(array, lax.axis_size(axis)), axis)


def split_high_low(array):
    high = array.astype(BF16)
    return high, (array - high.astype(F32)).astype(BF16)


def side_by_side(query, output):
    half = query.shape[-2] // 2
    return jnp.concatenate(
        [query[..., :half, :], output[..., :half, :], query[..., half:, :], output[..., half:, :]],
        axis=-1,
    )


def in_plane(rows, cols, core):
    side = 4
    pairs = []
    for y in range(side):
        for x in range(side):
            for c in range(2):
                to = ((y + rows) % side * side + (x + cols) % side) * 2 + (c + core) % 2
                pairs.append(((y * side + x) * 2 + c, to))
    return pairs


def send(array, rows, cols, core=0):
    return lax.ppermute(array, "shard", in_plane(rows, cols, core))


def by_exchange(cotan):
    side = 4
    rows = [[(y * side + x) * 2 + c for x in range(side)] for y in range(side) for c in range(2)]
    cols = [[(y * side + x) * 2 + c for y in range(side)] for x in range(side) for c in range(2)]
    row = exchange(copies(cotan.T, side), "shard", rows)
    return exchange(copies(row, side), "shard", cols)


def by_rings(cotan):
    block = cotan.T
    below, above, across = send(block, 1, 0), send(block, 3, 0), send(block, 2, 0)
    column = jnp.stack([block, above, across, below])
    left, right = send(column, 0, 1), send(column, 0, 3)
    half = column.shape[0] // 2
    far_low, far_high = send(left[:half], 0, 1), send(right[half:], 0, 3)
    return column, right, far_low, far_high, left


def partner(array):
    return send(array, 0, 0, 1)


def gradient_kernel(factor, shard, *refs):
    acts_in, error_in, start_in, *sources = refs[:-11]
    full_out, left, acts, error, start, columns, full, given, near, done, sent = refs[-11:]
    in_rings = len(sources) > 2
    mine, theirs = sources[: len(sources) // 2], sources[len(sources) // 2 :]
    side, each = 4, columns.shape[1] // 8
    y0, x0, core = shard[0] // 8, shard[0] // 2 % side, shard[0] % 2

    def block(refs, j, k):
        if not in_rings:
            return refs[0].at[j, k]
        near, right, far_low, far_high, left = refs
        if k == 2:
            return (far_low if j < 2 else far_high).at[j % 2]
        return (near, right, None, left)[k].at[j]

    def fetch(j, k, other):
        x = (x0 + k) % side if in_rings else k
        at = (x * 2 + (1 - core if other else core)) * each
        return pltpu.make_async_copy(
            block(theirs if other else mine, j, k),
            columns.at[j, pl.ds(pl.multiple_of(at, 16), each), :],
            done.at[j, k * 2 + other],
        )

    def lanes(j):
        y = (y0 + j) % side if in_rings else j
        return pl.ds(pl.multiple_of(y * (8 * each), 128), 8 * each)

    def prior(j):
        return pltpu.make_async_copy(error_in.at[:, lanes(j)], error.at[j], near.at[j])

    def result(j):
        return pltpu.make_async_copy(full.at[j], full_out.at[:, lanes(j)], sent.at[j])

    first = pltpu.make_async_copy(acts_in, acts, given.at[0])
    second = pltpu.make_async_copy(start_in.at[factor], start, given.at[1])
    first.start()
    steps = [(k, other) for k in range(side) for other in range(2)]
    for j in range(side):
        for k, other in steps:
            fetch(j, k, other).start()
        prior(j).start()
        if j == 0:
            second.start()
    first.wait()
    total = jnp.zeros(left.shape, F32)
    for j in range(side):
        for k, other in steps:
            fetch(j, k, other).wait()
        prior(j).wait()
        if j == 0:
            second.wait()
        part = contract(acts[...], columns[j], (1, 1)) + error[j].astype(F32)
        full[j] = part
        result(j).start()
        high, low = split_high_low(part)
        rows = start[:, lanes(j)]
        total += contract(high, rows, (1, 1)) + contract(low, rows, (1, 1))
    left[...] = total
    for j in range(side):
        result(j).wait()


def full_gradient(inputs, error, factors, factor, mine, theirs, shard):
    rows, tokens = inputs.shape[::-1]
    width, rank = error.shape[-1], factors.shape[-1]
    anywhere = pl.BlockSpec(memory_space=pl.ANY)
    return pl.pallas_call(
        functools.partial(gradient_kernel, factor),
        out_shape=(
            jax.ShapeDtypeStruct((rows, width), F32),
            jax.ShapeDtypeStruct((rows, rank), F32),
        ),
        in_specs=[
            pl.BlockSpec(memory_space=pltpu.SMEM),
            *[anywhere] * (3 + len(mine) + len(theirs)),
        ],
        out_specs=(anywhere, pl.BlockSpec(memory_space=pltpu.VMEM)),
        scratch_shapes=[
            pltpu.VMEM((rows, tokens), BF16),
            pltpu.VMEM((4, rows, width // 4), BF16),
            pltpu.VMEM((rank, width), BF16),
            pltpu.VMEM((4, width // 4, tokens), BF16),
            pltpu.VMEM((4, rows, width // 4), F32),
            pltpu.SemaphoreType.DMA((2,)),
            pltpu.SemaphoreType.DMA((4,)),
            pltpu.SemaphoreType.DMA((4, 8)),
            pltpu.SemaphoreType.DMA((4,)),
        ],
    )(shard, inputs.T, error[0], jnp.swapaxes(factors, 1, 2), *mine, *theirs)


TILE = 16


def tile_of(group, block, blocks, per_shard):
    at = group * blocks + block
    return at // per_shard, at % per_shard * TILE


def term_kernel(scale, arrived, *refs):
    fulls_in, (sent, left_out, fulls, done) = refs[:-4], refs[-4:]
    copies_in = [pltpu.make_async_copy(a, fulls.at[i], done.at[i]) for i, a in enumerate(fulls_in)]
    for copy in copies_in:
        copy.start()
    total = arrived[0].astype(F32)
    for r in range(1, arrived.shape[0]):
        total += arrived[r].astype(F32)
    total = total * scale
    rank = total.shape[1] // 4
    lefts = [
        jnp.concatenate(
            [total[:, i * rank : (i + 1) * rank], total[:, (i + 2) * rank : (i + 3) * rank]], axis=0
        )
        for i in range(2)
    ]
    left_out[0] = lefts[0]
    left_out[1] = lefts[1]
    shards, depth = sent.shape[:2]
    share = depth - rank
    grams = []
    for left in lefts:
        gram = lax.dot_general(
            left, left, (((0,), (0,)), ((), ())), precision=HIGH, preferred_element_type=F32
        )
        grams.extend(split_high_low(gram))
    grams = jnp.concatenate(grams, axis=1)
    for s in range(shards):
        sent[s, share:, :] = grams
    blocks = fulls.shape[2] // 128
    per_shard = share // TILE
    for t in range(2 * rank // TILE * blocks, shards * per_shard):
        sent[t // per_shard, t % per_shard * TILE : (t % per_shard + 1) * TILE, :] = jnp.zeros(
            (TILE, 128), BF16
        )
    for i in range(2):
        copies_in[i].wait()
        high, low = split_high_low(lefts[i].T)
        both = jnp.concatenate([high, low], axis=0)
        for c in range(4):
            width = fulls.shape[2] // 4
            full_high, full_low = split_high_low(fulls[i, :, c * width : (c + 1) * width])
            product = contract(both, full_high, (1, 0))
            product = product[:rank] + product[rank:] + contract(high, full_low, (1, 0))
            product = product.astype(BF16)
            for g in range(rank // TILE):
                for b in range(width // 128):
                    s, at = tile_of(
                        i * (rank // TILE) + g, c * (width // 128) + b, blocks, per_shard
                    )
                    sent[s, at : at + TILE, :] = product[
                        g * TILE : (g + 1) * TILE, b * 128 : (b + 1) * 128
                    ]


def terms(arrived, query_full, output_full, replicas, shards):
    rows, width = query_full.shape
    rank = arrived.shape[-1] // 4
    tiles = 2 * rank // TILE * (width // 128)
    depth = -(-tiles // shards) * TILE + rank
    vmem = pl.BlockSpec(memory_space=pltpu.VMEM)
    anywhere = pl.BlockSpec(memory_space=pl.ANY)
    return pl.pallas_call(
        functools.partial(term_kernel, 1.0 / replicas),
        out_shape=(
            jax.ShapeDtypeStruct((shards, depth, 128), BF16),
            jax.ShapeDtypeStruct((2, rows, rank), F32),
        ),
        in_specs=[vmem, anywhere, anywhere],
        out_specs=(vmem, vmem),
        scratch_shapes=[
            pltpu.VMEM((2, rows, width), F32),
            pltpu.SemaphoreType.DMA((2,)),
        ],
    )(arrived, query_full, output_full)


def finish_kernel(replica, arrived, rows, query_weight, output_weight, *refs):
    fulls_in, errors_out = refs[:2], refs[2:4]
    weights_out, (fulls, cols, errors, done, sent) = refs[4:6], refs[6:]
    chunks = 4
    width = fulls.shape[2] // chunks
    here = [pl.ds(c * width, width) for c in range(chunks)]

    def prior(i, c):
        return pltpu.make_async_copy(
            fulls_in[i].at[:, here[c]], fulls.at[i, :, here[c]], done.at[i, c]
        )

    def result(i, c):
        return pltpu.make_async_copy(
            errors.at[i, :, here[c]], errors_out[i].at[0, :, here[c]], sent.at[i, c]
        )

    each = [(i, c) for i in range(2) for c in range(chunks)]
    for i, c in each:
        prior(i, c).start()
    blocks = fulls.shape[2] // 128
    groups = cols.shape[0] // TILE
    per_shard = arrived.shape[1] // TILE
    for g in range(groups):
        for b in range(blocks):
            s, at = tile_of(g, b, blocks, per_shard)
            cols[g * TILE : (g + 1) * TILE, b * 128 : (b + 1) * 128] = arrived[s, at : at + TILE, :]
    rank = cols.shape[0] // 2
    for i, c in each:
        right = cols[i * rank : (i + 1) * rank, here[c]]
        approx = contract(rows[i], jnp.concatenate([right, right], axis=0), (1, 0))
        prior(i, c).wait()
        errors[i, :, here[c]] = (fulls[i, :, here[c]] - approx).astype(BF16)
        result(i, c).start()
    span = query_weight.shape[1]
    window = 384
    at = replica[0] * span
    base = jnp.minimum(at // 128 * 128, fulls.shape[2] - window)
    own = cols[:, pl.ds(pl.multiple_of(base, 128), window)].astype(F32)
    own = pltpu.roll(own, window - (at - base), 1)[:, :span].astype(BF16)
    for i, weight in enumerate((query_weight, output_weight)):
        right = own[i * rank : (i + 1) * rank]
        approx = contract(rows[i], jnp.concatenate([right, right], axis=0), (1, 0))
        weights_out[i][...] = weight[...] - approx
    for i, c in each:
        result(i, c).wait()


def finish(arrived, rows, fulls, weights, replica):
    height, width = fulls[0].shape
    rank = rows.shape[-1] // 2
    vmem = pl.BlockSpec(memory_space=pltpu.VMEM)
    anywhere = pl.BlockSpec(memory_space=pl.ANY)
    return pl.pallas_call(
        finish_kernel,
        out_shape=(
            *[jax.ShapeDtypeStruct((1, height, width), BF16)] * 2,
            *[jax.ShapeDtypeStruct(weights[0].shape, F32)] * 2,
        ),
        in_specs=[
            pl.BlockSpec(memory_space=pltpu.SMEM),
            vmem,
            vmem,
            vmem,
            vmem,
            anywhere,
            anywhere,
        ],
        out_specs=(anywhere, anywhere, vmem, vmem),
        scratch_shapes=[
            pltpu.VMEM((2, height, width), F32),
            pltpu.VMEM((2 * rank, width), BF16),
            pltpu.VMEM((2, height, width), BF16),
            pltpu.SemaphoreType.DMA((2, 4)),
            pltpu.SemaphoreType.DMA((2, 4)),
        ],
    )(replica, arrived, rows, *weights, *fulls)


def contract(a, b, dims):
    return lax.dot_general(a, b, ((dims[:1], dims[1:]), ((), ())), preferred_element_type=F32)


def inverse_factor(gram):
    chol = jnp.linalg.cholesky(gram)
    eye = jnp.eye(gram.shape[0], dtype=F32)
    return lax.linalg.triangular_solve(chol, eye, left_side=True, lower=True)


def step(
    hidden_in,
    context_in,
    query_cotan,
    output_cotan,
    query_error,
    output_error,
    query_weight,
    output_weight,
    start_factors,
):
    replicas = lax.axis_size("dp")
    shards = lax.axis_size("shard")
    shard = lax.axis_index("shard").reshape(1)
    replica = lax.axis_index("dp").reshape(1)
    query_mine = (by_exchange(query_cotan),)
    output_mine = by_rings(output_cotan)
    column, right, far_low, far_high, left = output_mine
    column = partner(column)
    right, left = partner(right), partner(left)
    far_low, far_high = partner(far_low), partner(far_high)
    query_theirs = [partner(a) for a in query_mine]
    output_full, output_left = full_gradient(
        context_in,
        output_error,
        start_factors,
        1,
        output_mine,
        (column, right, far_low, far_high, left),
        shard,
    )
    query_full, query_left = full_gradient(
        hidden_in, query_error, start_factors, 0, query_mine, query_theirs, shard
    )

    lefts = from_everyone(side_by_side(query_left, output_left).astype(BF16), "dp")
    sent, lefts = terms(lefts, query_full, output_full, replicas, shards)
    rank = lefts.shape[-1]
    arrived = exchange(sent, "shard").astype(F32).sum(axis=0)
    share, gram_parts = arrived[:-rank], arrived[-rank:]

    shares = from_everyone(share.astype(BF16), "dp")
    share = shares.astype(F32).sum(axis=0) / F32(replicas)

    def weighted(left, gram):
        inverse = inverse_factor(gram)
        ortho = lax.dot_general(left, inverse, (((1,), (1,)), ((), ())), precision=HIGH)
        high, low = split_high_low(jnp.dot(ortho, inverse, precision=HIGH))
        return jnp.concatenate([high, low], axis=1)

    query_rows = weighted(lefts[0], gram_parts[:, :rank] + gram_parts[:, rank : 2 * rank])
    output_rows = weighted(lefts[1], gram_parts[:, 2 * rank : 3 * rank] + gram_parts[:, 3 * rank :])
    cols = from_everyone(share.astype(BF16), "shard")
    return finish(
        cols,
        jnp.stack([query_rows, output_rows]),
        (query_full, output_full),
        (query_weight, output_weight),
        replica,
    )


def solution(mesh):
    placed = (
        P("dp", "shard"),
        P("dp", "shard"),
        P("dp", "shard"),
        P("dp", "shard"),
        P("dp", "shard", None),
        P("dp", "shard", None),
        P("shard", "dp"),
        P("shard", "dp"),
        P(),
    )
    return jax.shard_map(
        step,
        mesh=mesh,
        in_specs=placed,
        out_specs=(
            P("dp", "shard", None),
            P("dp", "shard", None),
            P("shard", "dp"),
            P("shard", "dp"),
        ),
        check_vma=False,
    )
```

```python
import functools

import jax
import jax.numpy as jnp
from jax import lax
from jax.experimental import pallas as pl
from jax.experimental.pallas import tpu as pltpu
from jax.sharding import PartitionSpec as P


HIGH = lax.Precision.HIGHEST
F32 = jnp.float32
BF16 = jnp.bfloat16


def copies(array, count):
    return jnp.broadcast_to(array, (count, *array.shape))


def exchange(array, axis, groups=None):
    return lax.all_to_all(array, axis, 0, 0, tiled=True, axis_index_groups=groups)


def from_everyone(array, axis):
    return exchange(copies(array, lax.axis_size(axis)), axis)


def split_high_low(array):
    high = array.astype(BF16)
    return high, (array - high.astype(F32)).astype(BF16)


def in_plane(rows, cols, core):
    side = 4
    pairs = []
    for y in range(side):
        for x in range(side):
            for c in range(2):
                to = ((y + rows) % side * side + (x + cols) % side) * 2 + (c + core) % 2
                pairs.append(((y * side + x) * 2 + c, to))
    return pairs


def send(array, rows, cols, core=0):
    return lax.ppermute(array, "shard", in_plane(rows, cols, core))


def by_exchange(cotan):
    side = 4
    rows = [[(y * side + x) * 2 + c for x in range(side)] for y in range(side) for c in range(2)]
    cols = [[(y * side + x) * 2 + c for y in range(side)] for x in range(side) for c in range(2)]
    row = exchange(copies(cotan.T, side), "shard", rows)
    return exchange(copies(row, side), "shard", cols)


def by_rings(cotan):
    block = cotan.T
    below, above, across = send(block, 1, 0), send(block, 3, 0), send(block, 2, 0)
    column = jnp.stack([block, above, across, below])
    left, right = send(column, 0, 1), send(column, 0, 3)
    half = column.shape[0] // 2
    far_low, far_high = send(left[:half], 0, 1), send(right[half:], 0, 3)
    return column, right, far_low, far_high, left


def partner(array):
    return send(array, 0, 0, 1)


def gradient_kernel(factor, shard, *refs):
    acts_in, error_in, start_in, *sources = refs[:-9]
    full, left, acts, error, start, columns, given, near, done = refs[-9:]
    in_rings = len(sources) > 3
    other_left = None if in_rings else sources.pop()
    mine, theirs = sources[: len(sources) // 2], sources[len(sources) // 2 :]
    side, each = 4, columns.shape[1] // 8
    y0, x0, core = shard[0] // 8, shard[0] // 2 % side, shard[0] % 2

    def block(refs, j, k):
        if not in_rings:
            return refs[0].at[j, k]
        near, right, far_low, far_high, left = refs
        if k == 2:
            return (far_low if j < 2 else far_high).at[j % 2]
        return (near, right, None, left)[k].at[j]

    def fetch(j, k, other):
        x = (x0 + k) % side if in_rings else k
        at = (x * 2 + (1 - core if other else core)) * each
        return pltpu.make_async_copy(
            block(theirs if other else mine, j, k),
            columns.at[j, pl.ds(pl.multiple_of(at, 16), each), :],
            done.at[j, k * 2 + other],
        )

    def lanes(j):
        y = (y0 + j) % side if in_rings else j
        return pl.ds(pl.multiple_of(y * (8 * each), 128), 8 * each)

    def prior(j):
        return pltpu.make_async_copy(error_in.at[:, lanes(j)], error.at[j], near.at[j])

    first = pltpu.make_async_copy(acts_in, acts, given.at[0])
    second = pltpu.make_async_copy(start_in.at[factor], start, given.at[1])
    first.start()
    steps = [(k, other) for k in range(side) for other in range(2)]
    for j in range(side):
        for k, other in steps:
            fetch(j, k, other).start()
        prior(j).start()
        if j == 0:
            second.start()
    first.wait()
    total = jnp.zeros((acts.shape[0], start.shape[0]), F32)
    for j in range(side):
        for k, other in steps:
            fetch(j, k, other).wait()
        prior(j).wait()
        if j == 0:
            second.wait()
        part = contract(acts[...], columns[j], (1, 1)) + error[j].astype(F32)
        full[:, lanes(j)] = part
        high, low = split_high_low(part)
        rows = start[:, lanes(j)]
        total += contract(high, rows, (1, 1)) + contract(low, rows, (1, 1))
    if in_rings:
        left[...] = total
    else:
        half = total.shape[0] // 2
        packed = jnp.concatenate(
            [total[:half], other_left[:half], total[half:], other_left[half:]], axis=1
        ).astype(BF16)
        for r in range(left.shape[0]):
            left[r] = packed


def in_vmem(*arrays):
    return [pltpu.with_memory_space_constraint(a, pltpu.VMEM) for a in arrays]


def in_hbm(*arrays):
    return [pltpu.with_memory_space_constraint(a, pltpu.HBM) for a in arrays]


def full_gradient(inputs, error, factors, factor, blocks, shard, left, *lefts):
    rows, tokens = inputs.shape[::-1]
    width = error.shape[-1]
    vmem = pl.BlockSpec(memory_space=pltpu.VMEM)
    return pl.pallas_call(
        functools.partial(gradient_kernel, factor),
        out_shape=(pltpu.VMEM((rows, width), F32), left),
        in_specs=[
            pl.BlockSpec(memory_space=pltpu.SMEM),
            *[pl.BlockSpec(memory_space=pltpu.HBM)] * 3,
            *[pl.BlockSpec(memory_space=pltpu.HBM)] * len(blocks),
            *[vmem] * len(lefts),
        ],
        out_specs=(vmem, vmem),
        scratch_shapes=[
            pltpu.VMEM((rows, tokens), BF16),
            pltpu.VMEM((4, rows, width // 4), BF16),
            pltpu.VMEM((factors.shape[-1], width), BF16),
            pltpu.VMEM((4, width // 4, tokens), BF16),
            pltpu.SemaphoreType.DMA((2,)),
            pltpu.SemaphoreType.DMA((4,)),
            pltpu.SemaphoreType.DMA((4, 8)),
        ],
        compiler_params=pltpu.CompilerParams(vmem_limit_bytes=20 << 20),
    )(shard, *in_hbm(inputs.T, error[0], jnp.swapaxes(factors, 1, 2), *blocks), *in_vmem(*lefts))


TILE = 16


def tile_of(group, block, blocks, per_shard):
    at = group * blocks + block
    return at // per_shard, at % per_shard * TILE


def term_kernel(scale, arrived, *refs):
    *fulls, sent, left_out = refs
    total = arrived[0].astype(F32)
    for r in range(1, arrived.shape[0]):
        total += arrived[r].astype(F32)
    total = total * scale
    rank = total.shape[1] // 4
    lefts = [
        jnp.concatenate(
            [total[:, i * rank : (i + 1) * rank], total[:, (i + 2) * rank : (i + 3) * rank]], axis=0
        )
        for i in range(2)
    ]
    left_out[0] = lefts[0]
    left_out[1] = lefts[1]
    shards, depth = sent.shape[:2]
    share = depth - rank
    grams = []
    for left in lefts:
        gram = lax.dot_general(
            left, left, (((0,), (0,)), ((), ())), precision=HIGH, preferred_element_type=F32
        )
        grams.extend(split_high_low(gram))
    grams = jnp.concatenate(grams, axis=1)
    for s in range(shards):
        sent[s, share:, :] = grams
    full_width = fulls[0].shape[1]
    blocks = full_width // 128
    per_shard = share // TILE
    for t in range(2 * rank // TILE * blocks, shards * per_shard):
        sent[t // per_shard, t % per_shard * TILE : (t % per_shard + 1) * TILE, :] = jnp.zeros(
            (TILE, 128), BF16
        )
    for i in range(2):
        high, low = split_high_low(lefts[i].T)
        both = jnp.concatenate([high, low], axis=0)
        for c in range(4):
            width = full_width // 4
            full_high, full_low = split_high_low(fulls[i][:, c * width : (c + 1) * width])
            product = contract(both, full_high, (1, 0))
            product = product[:rank] + product[rank:] + contract(high, full_low, (1, 0))
            product = product.astype(BF16)
            for g in range(rank // TILE):
                for b in range(width // 128):
                    s, at = tile_of(
                        i * (rank // TILE) + g, c * (width // 128) + b, blocks, per_shard
                    )
                    sent[s, at : at + TILE, :] = product[
                        g * TILE : (g + 1) * TILE, b * 128 : (b + 1) * 128
                    ]


def terms(arrived, query_full, output_full, replicas, shards):
    rows, width = query_full.shape
    rank = arrived.shape[-1] // 4
    tiles = 2 * rank // TILE * (width // 128)
    depth = -(-tiles // shards) * TILE + rank
    vmem = pl.BlockSpec(memory_space=pltpu.VMEM)
    return pl.pallas_call(
        functools.partial(term_kernel, 1.0 / replicas),
        out_shape=(
            jax.ShapeDtypeStruct((shards, depth, 128), BF16),
            jax.ShapeDtypeStruct((2, rows, rank), F32),
        ),
        in_specs=[vmem] * 3,
        out_specs=(vmem, vmem),
        compiler_params=pltpu.CompilerParams(vmem_limit_bytes=16 << 20),
    )(*in_vmem(arrived, query_full, output_full))


def finish_kernel(replica, arrived, rows, query_weight, output_weight, *refs):
    fulls, errors_out = refs[:2], refs[2:4]
    weights_out, (cols, errors, sent) = refs[4:6], refs[6:]
    chunks = 4
    full_width = cols.shape[1]
    width = full_width // chunks
    here = [pl.ds(c * width, width) for c in range(chunks)]

    def result(i, c):
        return pltpu.make_async_copy(
            errors.at[i, :, here[c]], errors_out[i].at[0, :, here[c]], sent.at[i, c]
        )

    each = [(i, c) for i in range(2) for c in range(chunks)]
    blocks = full_width // 128
    groups = cols.shape[0] // TILE
    per_shard = arrived.shape[1] // TILE
    for g in range(groups):
        for b in range(blocks):
            s, at = tile_of(g, b, blocks, per_shard)
            cols[g * TILE : (g + 1) * TILE, b * 128 : (b + 1) * 128] = arrived[s, at : at + TILE, :]
    rank = cols.shape[0] // 2
    for i, c in each:
        right = cols[i * rank : (i + 1) * rank, here[c]]
        approx = contract(rows[i], jnp.concatenate([right, right], axis=0), (1, 0))
        errors[i, :, here[c]] = (fulls[i][:, here[c]] - approx).astype(BF16)
        result(i, c).start()
    span = query_weight.shape[1]
    window = 384
    at = replica[0] * span
    base = jnp.minimum(at // 128 * 128, full_width - window)
    own = cols[:, pl.ds(pl.multiple_of(base, 128), window)].astype(F32)
    own = pltpu.roll(own, window - (at - base), 1)[:, :span].astype(BF16)
    for i, weight in enumerate((query_weight, output_weight)):
        right = own[i * rank : (i + 1) * rank]
        approx = contract(rows[i], jnp.concatenate([right, right], axis=0), (1, 0))
        weights_out[i][...] = weight[...] - approx
    for i, c in each:
        result(i, c).wait()


def finish(arrived, rows, fulls, weights, replica):
    height, width = fulls[0].shape
    rank = rows.shape[-1] // 2
    vmem = pl.BlockSpec(memory_space=pltpu.VMEM)
    anywhere = pl.BlockSpec(memory_space=pl.ANY)
    return pl.pallas_call(
        finish_kernel,
        out_shape=(
            *[jax.ShapeDtypeStruct((1, height, width), BF16)] * 2,
            *[jax.ShapeDtypeStruct(weights[0].shape, F32)] * 2,
        ),
        in_specs=[pl.BlockSpec(memory_space=pltpu.SMEM), *[vmem] * 6],
        out_specs=(anywhere, anywhere, vmem, vmem),
        scratch_shapes=[
            pltpu.VMEM((2 * rank, width), BF16),
            pltpu.VMEM((2, height, width), BF16),
            pltpu.SemaphoreType.DMA((2, 4)),
        ],
        compiler_params=pltpu.CompilerParams(vmem_limit_bytes=16 << 20),
    )(replica, *in_vmem(arrived), rows, *weights, *in_vmem(*fulls))


def contract(a, b, dims):
    return lax.dot_general(a, b, ((dims[:1], dims[1:]), ((), ())), preferred_element_type=F32)


def inverse_factor(gram):
    chol = jnp.linalg.cholesky(gram)
    eye = jnp.eye(gram.shape[0], dtype=F32)
    return lax.linalg.triangular_solve(chol, eye, left_side=True, lower=True)


def step(
    hidden_in,
    context_in,
    query_cotan,
    output_cotan,
    query_error,
    output_error,
    query_weight,
    output_weight,
    start_factors,
):
    replicas = lax.axis_size("dp")
    shards = lax.axis_size("shard")
    shard = lax.axis_index("shard").reshape(1)
    replica = lax.axis_index("dp").reshape(1)
    query_mine = (by_exchange(query_cotan),)
    output_mine = by_rings(output_cotan)
    column, right, far_low, far_high, left = output_mine
    column = partner(column)
    right, left = partner(right), partner(left)
    far_low, far_high = partner(far_low), partner(far_high)
    query_theirs = [partner(a) for a in query_mine]
    rows, rank = output_error.shape[1], start_factors.shape[-1]
    output_full, output_left = full_gradient(
        context_in,
        output_error,
        start_factors,
        1,
        (*output_mine, column, right, far_low, far_high, left),
        shard,
        pltpu.VMEM((rows, rank), F32),
    )
    query_full, lefts = full_gradient(
        hidden_in,
        query_error,
        start_factors,
        0,
        (*query_mine, *query_theirs),
        shard,
        pltpu.VMEM((replicas, rows // 2, 4 * rank), BF16),
        output_left,
    )

    sent, lefts = terms(exchange(lefts, "dp"), query_full, output_full, replicas, shards)
    arrived = exchange(sent, "shard").astype(F32).sum(axis=0)
    share, gram_parts = arrived[:-rank], arrived[-rank:]

    shares = from_everyone(share.astype(BF16), "dp")
    share = shares.astype(F32).sum(axis=0) / F32(replicas)

    def weighted(left, gram):
        inverse = inverse_factor(gram)
        ortho = lax.dot_general(left, inverse, (((1,), (1,)), ((), ())), precision=HIGH)
        high, low = split_high_low(jnp.dot(ortho, inverse, precision=HIGH))
        return jnp.concatenate([high, low], axis=1)

    query_rows = weighted(lefts[0], gram_parts[:, :rank] + gram_parts[:, rank : 2 * rank])
    output_rows = weighted(lefts[1], gram_parts[:, 2 * rank : 3 * rank] + gram_parts[:, 3 * rank :])
    cols = from_everyone(share.astype(BF16), "shard")
    return finish(
        cols,
        jnp.stack([query_rows, output_rows]),
        (query_full, output_full),
        (query_weight, output_weight),
        replica,
    )


def solution(mesh):
    placed = (
        P("dp", "shard"),
        P("dp", "shard"),
        P("dp", "shard"),
        P("dp", "shard"),
        P("dp", "shard", None),
        P("dp", "shard", None),
        P("shard", "dp"),
        P("shard", "dp"),
        P(),
    )
    return jax.shard_map(
        step,
        mesh=mesh,
        in_specs=placed,
        out_specs=(
            P("dp", "shard", None),
            P("dp", "shard", None),
            P("shard", "dp"),
            P("shard", "dp"),
        ),
        check_vma=False,
    )
```

```python
import functools

import jax
import jax.numpy as jnp
from jax import lax
from jax.experimental import pallas as pl
from jax.experimental.pallas import tpu as pltpu
from jax.sharding import PartitionSpec as P


HIGH = lax.Precision.HIGHEST
F32 = jnp.float32
BF16 = jnp.bfloat16


def copies(array, count):
    return jnp.broadcast_to(array, (count, *array.shape))


def exchange(array, axis, groups=None):
    return lax.all_to_all(array, axis, 0, 0, tiled=True, axis_index_groups=groups)


def from_everyone(array, axis):
    return exchange(copies(array, lax.axis_size(axis)), axis)


def split_high_low(array):
    high = array.astype(BF16)
    return high, (array - high.astype(F32)).astype(BF16)


def in_plane(rows, cols, core):
    side = 4
    pairs = []
    for y in range(side):
        for x in range(side):
            for c in range(2):
                to = ((y + rows) % side * side + (x + cols) % side) * 2 + (c + core) % 2
                pairs.append(((y * side + x) * 2 + c, to))
    return pairs


def send(array, rows, cols, core=0):
    return lax.ppermute(array, "shard", in_plane(rows, cols, core))


def ring(block, rows, cols):
    low, high = send(block, rows, cols), send(block, 3 * rows, 3 * cols)
    half = block.shape[0] // 2
    far = send(low[:half], rows, cols), send(high[half:], 3 * rows, 3 * cols)
    return block, high, *far, low


def first_ring(cotan, rows, cols):
    block = cotan.T
    low, high = send(block, rows, cols), send(block, 3 * rows, 3 * cols)
    far = send(block, 2 * rows, 2 * cols)
    return jnp.stack([block, high, far, low])


def partner(array):
    return send(array, 0, 0, 1)


def gradient_kernel(across, shard, *refs):
    acts_in, error_in, *sources = refs[:-7]
    full, acts, error, columns, given, near, done = refs[-7:]
    mine, theirs = sources[: len(sources) // 2], sources[len(sources) // 2 :]
    side, each = 4, columns.shape[1] // 8
    y0, x0, core = shard[0] // 8, shard[0] // 2 % side, shard[0] % 2

    def block(refs, j, k):
        outer, inner = (k, j) if across else (j, k)
        near, high, far_low, far_high, low = refs
        if outer == 2:
            return (far_low if inner < 2 else far_high).at[inner % 2]
        return (near, high, None, low)[outer].at[inner]

    def fetch(j, k, other):
        x = (x0 + k) % side
        at = (x * 2 + (1 - core if other else core)) * each
        return pltpu.make_async_copy(
            block(theirs if other else mine, j, k),
            columns.at[j, pl.ds(pl.multiple_of(at, 16), each), :],
            done.at[j, k * 2 + other],
        )

    def lanes(j):
        y = (y0 + j) % side
        return pl.ds(pl.multiple_of(y * (8 * each), 128), 8 * each)

    def prior(j):
        return pltpu.make_async_copy(error_in.at[:, lanes(j)], error.at[j], near.at[j])

    first = pltpu.make_async_copy(acts_in, acts, given.at[0])
    first.start()
    steps = [(k, other) for k in range(side) for other in range(2)]
    for j in range(side):
        for k, other in steps:
            fetch(j, k, other).start()
        prior(j).start()
    first.wait()
    for j in range(side):
        for k, other in steps:
            fetch(j, k, other).wait()
        prior(j).wait()
        full[:, lanes(j)] = contract(acts[...], columns[j], (1, 1)) + error[j].astype(F32)


def in_vmem(*arrays):
    return [pltpu.with_memory_space_constraint(a, pltpu.VMEM) for a in arrays]


def in_hbm(*arrays):
    return [pltpu.with_memory_space_constraint(a, pltpu.HBM) for a in arrays]


def full_gradient(inputs, error, blocks, shard, across):
    rows, tokens = inputs.shape[::-1]
    width = error.shape[-1]
    vmem = pl.BlockSpec(memory_space=pltpu.VMEM)
    return pl.pallas_call(
        functools.partial(gradient_kernel, across),
        out_shape=pltpu.VMEM((rows, width), F32),
        in_specs=[
            pl.BlockSpec(memory_space=pltpu.SMEM),
            *[pl.BlockSpec(memory_space=pltpu.HBM)] * (2 + len(blocks)),
        ],
        out_specs=vmem,
        scratch_shapes=[
            pltpu.VMEM((rows, tokens), BF16),
            pltpu.VMEM((4, rows, width // 4), BF16),
            pltpu.VMEM((4, width // 4, tokens), BF16),
            pltpu.SemaphoreType.DMA((1,)),
            pltpu.SemaphoreType.DMA((4,)),
            pltpu.SemaphoreType.DMA((4, 8)),
        ],
        compiler_params=pltpu.CompilerParams(vmem_limit_bytes=20 << 20),
    )(shard, *in_hbm(inputs.T, error[0], *blocks))


def inverse_kernel(grams, lefts, rows):
    rank = grams.shape[0]
    lane = lax.broadcasted_iota(jnp.int32, (rank, 4 * rank), 1)
    row = lax.broadcasted_iota(jnp.int32, (rank, 4 * rank), 0)
    given = grams[...]
    unit = (row[:, :rank] == lane[:, :rank]).astype(F32)
    state = jnp.concatenate(
        [
            given[:, :rank] + given[:, rank : 2 * rank],
            unit,
            given[:, 2 * rank : 3 * rank] + given[:, 3 * rank :],
            unit,
        ],
        axis=1,
    )
    query = lane < 2 * rank
    for k in range(rank):
        column = jnp.where(
            query, state[:, k : k + 1], state[:, 2 * rank + k : 2 * rank + k + 1]
        )
        pivot = state[k : k + 1, :] / column[k : k + 1, :]
        state = jnp.where(row == k, pivot, state - column * pivot)
    for i in range(2):
        inverse = state[:, (2 * i + 1) * rank : (2 * i + 2) * rank]
        product = jnp.dot(lefts[i], inverse, precision=HIGH, preferred_element_type=F32)
        rows[i] = jnp.concatenate(split_high_low(product), axis=1)


def weighted_lefts(grams, lefts):
    vmem = pl.BlockSpec(memory_space=pltpu.VMEM)
    return pl.pallas_call(
        inverse_kernel,
        out_shape=pltpu.VMEM((*lefts.shape[:2], 2 * lefts.shape[2]), BF16),
        in_specs=[vmem, vmem],
        out_specs=vmem,
        compiler_params=pltpu.CompilerParams(vmem_limit_bytes=8 << 20),
    )(grams, lefts)


TILE = 16


def tile_of(group, block, blocks, per_shard):
    at = group * blocks + block
    return at // per_shard, at % per_shard * TILE


def term_kernel(scale, arrived, *refs):
    *fulls, sent, left_out = refs
    total = arrived[0].astype(F32)
    for r in range(1, arrived.shape[0]):
        total += arrived[r].astype(F32)
    total = total * scale
    rank = total.shape[1] // 4
    lefts = [
        jnp.concatenate(
            [total[:, i * rank : (i + 1) * rank], total[:, (i + 2) * rank : (i + 3) * rank]], axis=0
        )
        for i in range(2)
    ]
    left_out[0] = lefts[0]
    left_out[1] = lefts[1]
    shards, depth = sent.shape[:2]
    share = depth - rank
    grams = []
    for left in lefts:
        gram = lax.dot_general(
            left, left, (((0,), (0,)), ((), ())), precision=HIGH, preferred_element_type=F32
        )
        grams.extend(split_high_low(gram))
    grams = jnp.concatenate(grams, axis=1)
    for s in range(shards):
        sent[s, share:, :] = grams
    full_width = fulls[0].shape[1]
    blocks = full_width // 128
    per_shard = share // TILE
    for t in range(2 * rank // TILE * blocks, shards * per_shard):
        sent[t // per_shard, t % per_shard * TILE : (t % per_shard + 1) * TILE, :] = jnp.zeros(
            (TILE, 128), BF16
        )
    for i in range(2):
        high, low = split_high_low(lefts[i].T)
        both = jnp.concatenate([high, low], axis=0)
        for c in range(4):
            width = full_width // 4
            full_high, full_low = split_high_low(fulls[i][:, c * width : (c + 1) * width])
            product = contract(both, full_high, (1, 0))
            product = product[:rank] + product[rank:] + contract(high, full_low, (1, 0))
            product = product.astype(BF16)
            for g in range(rank // TILE):
                for b in range(width // 128):
                    s, at = tile_of(
                        i * (rank // TILE) + g, c * (width // 128) + b, blocks, per_shard
                    )
                    sent[s, at : at + TILE, :] = product[
                        g * TILE : (g + 1) * TILE, b * 128 : (b + 1) * 128
                    ]


def terms(arrived, query_full, output_full, replicas, shards):
    rows, width = query_full.shape
    rank = arrived.shape[-1] // 4
    tiles = 2 * rank // TILE * (width // 128)
    depth = -(-tiles // shards) * TILE + rank
    vmem = pl.BlockSpec(memory_space=pltpu.VMEM)
    return pl.pallas_call(
        functools.partial(term_kernel, 1.0 / replicas),
        out_shape=(
            pltpu.HBM((shards, depth, 128), BF16),
            pltpu.HBM((2, rows, rank), F32),
        ),
        in_specs=[vmem] * 3,
        out_specs=(vmem, vmem),
        compiler_params=pltpu.CompilerParams(vmem_limit_bytes=16 << 20),
    )(*in_vmem(arrived, query_full, output_full))


def finish_kernel(replica, arrived, rows, query_weight, output_weight, *refs):
    fulls, errors_out = refs[:2], refs[2:4]
    weights_out, (cols, errors, sent) = refs[4:6], refs[6:]
    chunks = 4
    full_width = cols.shape[1]
    width = full_width // chunks
    here = [pl.ds(c * width, width) for c in range(chunks)]

    def result(i, c):
        return pltpu.make_async_copy(
            errors.at[i, :, here[c]], errors_out[i].at[0, :, here[c]], sent.at[i, c]
        )

    each = [(i, c) for i in range(2) for c in range(chunks)]
    blocks = full_width // 128
    groups = cols.shape[0] // TILE
    per_shard = arrived.shape[1] // TILE
    for g in range(groups):
        for b in range(blocks):
            s, at = tile_of(g, b, blocks, per_shard)
            cols[g * TILE : (g + 1) * TILE, b * 128 : (b + 1) * 128] = arrived[s, at : at + TILE, :]
    rank = cols.shape[0] // 2
    for i, c in each:
        right = cols[i * rank : (i + 1) * rank, here[c]]
        approx = contract(rows[i], jnp.concatenate([right, right], axis=0), (1, 0))
        errors[i, :, here[c]] = (fulls[i][:, here[c]] - approx).astype(BF16)
        result(i, c).start()
    span = query_weight.shape[1]
    window = 384
    at = replica[0] * span
    base = jnp.minimum(at // 128 * 128, full_width - window)
    own = cols[:, pl.ds(pl.multiple_of(base, 128), window)].astype(F32)
    own = pltpu.roll(own, window - (at - base), 1)[:, :span].astype(BF16)
    for i, weight in enumerate((query_weight, output_weight)):
        right = own[i * rank : (i + 1) * rank]
        approx = contract(rows[i], jnp.concatenate([right, right], axis=0), (1, 0))
        weights_out[i][...] = weight[...] - approx
    for i, c in each:
        result(i, c).wait()


def finish(arrived, rows, fulls, weights, replica):
    height, width = fulls[0].shape
    rank = rows.shape[-1] // 2
    vmem = pl.BlockSpec(memory_space=pltpu.VMEM)
    anywhere = pl.BlockSpec(memory_space=pl.ANY)
    return pl.pallas_call(
        finish_kernel,
        out_shape=(
            *[jax.ShapeDtypeStruct((1, height, width), BF16)] * 2,
            *[jax.ShapeDtypeStruct(weights[0].shape, F32)] * 2,
        ),
        in_specs=[pl.BlockSpec(memory_space=pltpu.SMEM), *[vmem] * 6],
        out_specs=(anywhere, anywhere, vmem, vmem),
        scratch_shapes=[
            pltpu.VMEM((2 * rank, width), BF16),
            pltpu.VMEM((2, height, width), BF16),
            pltpu.SemaphoreType.DMA((2, 4)),
        ],
        compiler_params=pltpu.CompilerParams(vmem_limit_bytes=16 << 20),
    )(replica, *in_vmem(arrived), rows, *weights, *in_vmem(*fulls))


def contract(a, b, dims):
    return lax.dot_general(a, b, ((dims[:1], dims[1:]), ((), ())), preferred_element_type=F32)


def step(
    hidden_in,
    context_in,
    query_cotan,
    output_cotan,
    query_error,
    output_error,
    query_weight,
    output_weight,
    start_factors,
):
    replicas = lax.axis_size("dp")
    shards = lax.axis_size("shard")
    shard = lax.axis_index("shard").reshape(1)
    replica = lax.axis_index("dp").reshape(1)
    rows, rank = output_error.shape[1], start_factors.shape[-1]
    tokens, columns = query_cotan.shape

    own = lax.dynamic_slice_in_dim(start_factors, shard[0] * columns, columns, 1)
    partial = jnp.concatenate(
        [
            lax.dot_general(
                own[i], cotan, (((0,), (1,)), ((), ())), preferred_element_type=F32
            )
            for i, cotan in enumerate((query_cotan, output_cotan))
        ]
    )
    groups = partial.shape[0] // TILE
    tiles = partial.reshape(groups, TILE, -1, 128).swapaxes(1, 2).reshape(shards, -1, 128)
    tiles = exchange(tiles, "shard")
    tile = tiles.sum(axis=0)
    tiles = from_everyone(tile, "shard")
    whole = tiles.reshape(groups, -1, TILE, 128).swapaxes(1, 2).reshape(2, rank, tokens)

    query_line = first_ring(query_cotan, 0, 1)
    output_line = first_ring(output_cotan, 1, 0)

    def left_of(inputs, error, projection):
        prior = contract(error[0], start_factors[projection], (1, 0))
        prior = lax.optimization_barrier(prior)
        high, low = split_high_low(whole[projection])
        return contract(inputs.T, high, (1, 1)) + contract(inputs.T, low, (1, 1)) + prior

    query_left = left_of(hidden_in, query_error, 0)
    output_left = left_of(context_in, output_error, 1)
    half = rows // 2
    packed = jnp.concatenate(
        [query_left[:half], output_left[:half], query_left[half:], output_left[half:]], axis=1
    )
    lefts = from_everyone(packed.astype(BF16), "dp")

    output_mine = ring(output_line, 0, 1)
    query_mine = ring(query_line, 1, 0)

    def swapped(pieces):
        near, high, far_low, far_high, low = pieces
        near = partner(near)
        high, low = partner(high), partner(low)
        far_low, far_high = partner(far_low), partner(far_high)
        return near, high, far_low, far_high, low

    output_theirs = swapped(output_mine)
    query_theirs = swapped(query_mine)
    output_full = full_gradient(
        context_in, output_error, (*output_mine, *output_theirs), shard, True
    )
    query_full = full_gradient(hidden_in, query_error, (*query_mine, *query_theirs), shard, False)

    sent, lefts = terms(lefts, query_full, output_full, replicas, shards)
    arrived = exchange(sent, "shard").astype(F32).sum(axis=0)
    share, grams = arrived[:-rank], arrived[-rank:]

    shares = from_everyone(share.astype(BF16), "dp")
    share = shares.astype(F32).sum(axis=0) / F32(replicas)

    weighted = weighted_lefts(grams, lefts)
    cols = from_everyone(share.astype(BF16), "shard")
    return finish(
        cols,
        weighted,
        (query_full, output_full),
        (query_weight, output_weight),
        replica,
    )


def solution(mesh):
    placed = (
        P("dp", "shard"),
        P("dp", "shard"),
        P("dp", "shard"),
        P("dp", "shard"),
        P("dp", "shard", None),
        P("dp", "shard", None),
        P("shard", "dp"),
        P("shard", "dp"),
        P(),
    )
    return jax.shard_map(
        step,
        mesh=mesh,
        in_specs=placed,
        out_specs=(
            P("dp", "shard", None),
            P("dp", "shard", None),
            P("shard", "dp"),
            P("shard", "dp"),
        ),
        check_vma=False,
    )
```

```python
import functools

import jax
import jax.numpy as jnp
from jax import lax
from jax.experimental import pallas as pl
from jax.experimental.pallas import tpu as pltpu
from jax.sharding import PartitionSpec as P


HIGH = lax.Precision.HIGHEST
F32 = jnp.float32
BF16 = jnp.bfloat16


def copies(array, count):
    return jnp.broadcast_to(array, (count, *array.shape))


def exchange(array, axis, groups=None):
    return lax.all_to_all(array, axis, 0, 0, tiled=True, axis_index_groups=groups)


def split_high_low(array):
    high = array.astype(BF16)
    return high, (array - high.astype(F32)).astype(BF16)


def in_plane(rows, cols, core):
    side = 4
    pairs = []
    for y in range(side):
        for x in range(side):
            for c in range(2):
                to = ((y + rows) % side * side + (x + cols) % side) * 2 + (c + core) % 2
                pairs.append(((y * side + x) * 2 + c, to))
    return pairs


def send(array, rows, cols, core=0):
    return lax.ppermute(array, "shard", in_plane(rows, cols, core))


def by_exchange(cotan):
    side = 4
    rows = [[(y * side + x) * 2 + c for x in range(side)] for y in range(side) for c in range(2)]
    cols = [[(y * side + x) * 2 + c for y in range(side)] for x in range(side) for c in range(2)]
    row = exchange(copies(cotan.T, side), "shard", rows)
    return exchange(copies(row, side), "shard", cols)


def by_rings(cotan):
    block = cotan.T
    below, above, across = send(block, 1, 0), send(block, 3, 0), send(block, 2, 0)
    column = jnp.stack([block, above, across, below])
    left, right = send(column, 0, 1), send(column, 0, 3)
    half = column.shape[0] // 2
    far_low, far_high = send(left[:half], 0, 1), send(right[half:], 0, 3)
    return column, right, far_low, far_high, left


def partner(array):
    return send(array, 0, 0, 1)


def gradient_kernel(factor, shard, *refs):
    acts_in, error_in, start_in, *sources = refs[:-9]
    full, left, acts, error, start, columns, given, near, done = refs[-9:]
    in_rings = len(sources) > 3
    other_left = None if in_rings else sources.pop()
    mine, theirs = sources[: len(sources) // 2], sources[len(sources) // 2 :]
    side, each = 4, columns.shape[1] // 8
    y0, x0, core = shard[0] // 8, shard[0] // 2 % side, shard[0] % 2

    def block(refs, j, k):
        if not in_rings:
            return refs[0].at[j, k]
        near, right, far_low, far_high, left = refs
        if k == 2:
            return (far_low if j < 2 else far_high).at[j % 2]
        return (near, right, None, left)[k].at[j]

    def fetch(j, k, other):
        x = (x0 + k) % side if in_rings else k
        at = (x * 2 + (1 - core if other else core)) * each
        return pltpu.make_async_copy(
            block(theirs if other else mine, j, k),
            columns.at[j, pl.ds(pl.multiple_of(at, 16), each), :],
            done.at[j, k * 2 + other],
        )

    def lanes(j):
        y = (y0 + j) % side if in_rings else j
        return pl.ds(pl.multiple_of(y * (8 * each), 128), 8 * each)

    def prior(j):
        return pltpu.make_async_copy(error_in.at[:, lanes(j)], error.at[j], near.at[j])

    first = pltpu.make_async_copy(acts_in, acts, given.at[0])
    second = pltpu.make_async_copy(start_in.at[factor], start, given.at[1])
    first.start()
    steps = [(k, other) for k in range(side) for other in range(2)]
    for j in range(side):
        for k, other in steps:
            fetch(j, k, other).start()
        prior(j).start()
        if j == 0:
            second.start()
    first.wait()
    total = jnp.zeros((acts.shape[0], start.shape[0]), F32)
    for j in range(side):
        for k, other in steps:
            fetch(j, k, other).wait()
        prior(j).wait()
        if j == 0:
            second.wait()
        part = contract(acts[...], columns[j], (1, 1)) + error[j].astype(F32)
        full[:, lanes(j)] = part
        high, low = split_high_low(part)
        rows = start[:, lanes(j)]
        total += contract(high, rows, (1, 1)) + contract(low, rows, (1, 1))
    if in_rings:
        left[...] = total
    else:
        half = total.shape[0] // 2
        packed = jnp.concatenate(
            [total[:half], other_left[:half], total[half:], other_left[half:]], axis=1
        ).astype(BF16)
        for r in range(left.shape[0]):
            left[r] = packed


def in_vmem(*arrays):
    return [pltpu.with_memory_space_constraint(a, pltpu.VMEM) for a in arrays]


def in_hbm(*arrays):
    return [pltpu.with_memory_space_constraint(a, pltpu.HBM) for a in arrays]


def full_gradient(inputs, error, factors, factor, blocks, shard, left, *lefts):
    rows, tokens = inputs.shape[::-1]
    width = error.shape[-1]
    vmem = pl.BlockSpec(memory_space=pltpu.VMEM)
    return pl.pallas_call(
        functools.partial(gradient_kernel, factor),
        out_shape=(pltpu.VMEM((rows, width), F32), left),
        in_specs=[
            pl.BlockSpec(memory_space=pltpu.SMEM),
            *[pl.BlockSpec(memory_space=pltpu.HBM)] * 3,
            *[pl.BlockSpec(memory_space=pltpu.HBM)] * len(blocks),
            *[vmem] * len(lefts),
        ],
        out_specs=(vmem, vmem),
        scratch_shapes=[
            pltpu.VMEM((rows, tokens), BF16),
            pltpu.VMEM((4, rows, width // 4), BF16),
            pltpu.VMEM((factors.shape[-1], width), BF16),
            pltpu.VMEM((4, width // 4, tokens), BF16),
            pltpu.SemaphoreType.DMA((2,)),
            pltpu.SemaphoreType.DMA((4,)),
            pltpu.SemaphoreType.DMA((4, 8)),
        ],
        compiler_params=pltpu.CompilerParams(vmem_limit_bytes=20 << 20),
    )(shard, *in_hbm(inputs.T, error[0], jnp.swapaxes(factors, 1, 2), *blocks), *in_vmem(*lefts))


def inverse_kernel(grams, lefts, rows):
    rank = grams.shape[0]
    lane = lax.broadcasted_iota(jnp.int32, (rank, 4 * rank), 1)
    row = lax.broadcasted_iota(jnp.int32, (rank, 4 * rank), 0)
    given = grams[...]
    unit = (row[:, :rank] == lane[:, :rank]).astype(F32)
    state = jnp.concatenate(
        [
            given[:, :rank] + given[:, rank : 2 * rank],
            unit,
            given[:, 2 * rank : 3 * rank] + given[:, 3 * rank :],
            unit,
        ],
        axis=1,
    )
    query = lane < 2 * rank
    for k in range(rank):
        column = jnp.where(
            query, state[:, k : k + 1], state[:, 2 * rank + k : 2 * rank + k + 1]
        )
        pivot = state[k : k + 1, :] / column[k : k + 1, :]
        state = jnp.where(row == k, pivot, state - column * pivot)
    for i in range(2):
        inverse = state[:, (2 * i + 1) * rank : (2 * i + 2) * rank]
        product = jnp.dot(lefts[i], inverse, precision=HIGH, preferred_element_type=F32)
        rows[i] = jnp.concatenate(split_high_low(product), axis=1)


def weighted_lefts(grams, lefts):
    vmem = pl.BlockSpec(memory_space=pltpu.VMEM)
    return pl.pallas_call(
        inverse_kernel,
        out_shape=pltpu.VMEM((*lefts.shape[:2], 2 * lefts.shape[2]), BF16),
        in_specs=[vmem, vmem],
        out_specs=vmem,
        compiler_params=pltpu.CompilerParams(vmem_limit_bytes=8 << 20),
    )(grams, lefts)


TILE = 16


def tile_of(group, block, blocks, per_shard):
    at = group * blocks + block
    return at // per_shard, at % per_shard * TILE


def sum_kernel(scale, arrived, copies_out, *rest):
    total = arrived[0].astype(F32)
    for r in range(1, arrived.shape[0]):
        total += arrived[r].astype(F32)
    depth = copies_out.shape[1]
    share = (total[:depth] * scale).astype(BF16)
    for r in range(copies_out.shape[0]):
        copies_out[r] = share
    for kept in rest:
        kept[...] = total[depth:]


def summed(arrived, receivers, depth, scale):
    vmem = pl.BlockSpec(memory_space=pltpu.VMEM)
    kept = arrived.shape[1] - depth
    out = [pltpu.HBM((receivers, depth, 128), BF16)]
    if kept:
        out.append(pltpu.HBM((kept, 128), F32))
    return pl.pallas_call(
        functools.partial(sum_kernel, scale),
        out_shape=out,
        in_specs=[vmem],
        out_specs=[vmem] * len(out),
        compiler_params=pltpu.CompilerParams(vmem_limit_bytes=8 << 20),
    )(arrived)


def term_kernel(scale, arrived, *refs):
    *fulls, sent, left_out = refs
    total = arrived[0].astype(F32)
    for r in range(1, arrived.shape[0]):
        total += arrived[r].astype(F32)
    total = total * scale
    rank = total.shape[1] // 4
    lefts = [
        jnp.concatenate(
            [total[:, i * rank : (i + 1) * rank], total[:, (i + 2) * rank : (i + 3) * rank]], axis=0
        )
        for i in range(2)
    ]
    left_out[0] = lefts[0]
    left_out[1] = lefts[1]
    shards, depth = sent.shape[:2]
    share = depth - rank
    grams = []
    for left in lefts:
        gram = lax.dot_general(
            left, left, (((0,), (0,)), ((), ())), precision=HIGH, preferred_element_type=F32
        )
        grams.extend(split_high_low(gram))
    grams = jnp.concatenate(grams, axis=1)
    for s in range(shards):
        sent[s, share:, :] = grams
    full_width = fulls[0].shape[1]
    blocks = full_width // 128
    per_shard = share // TILE
    for t in range(2 * rank // TILE * blocks, shards * per_shard):
        sent[t // per_shard, t % per_shard * TILE : (t % per_shard + 1) * TILE, :] = jnp.zeros(
            (TILE, 128), BF16
        )
    for i in range(2):
        high, low = split_high_low(lefts[i].T)
        both = jnp.concatenate([high, low], axis=0)
        for c in range(4):
            width = full_width // 4
            full_high, full_low = split_high_low(fulls[i][:, c * width : (c + 1) * width])
            product = contract(both, full_high, (1, 0))
            product = product[:rank] + product[rank:] + contract(high, full_low, (1, 0))
            product = product.astype(BF16)
            for g in range(rank // TILE):
                for b in range(width // 128):
                    s, at = tile_of(
                        i * (rank // TILE) + g, c * (width // 128) + b, blocks, per_shard
                    )
                    sent[s, at : at + TILE, :] = product[
                        g * TILE : (g + 1) * TILE, b * 128 : (b + 1) * 128
                    ]


def terms(arrived, query_full, output_full, replicas, shards):
    rows, width = query_full.shape
    rank = arrived.shape[-1] // 4
    tiles = 2 * rank // TILE * (width // 128)
    depth = -(-tiles // shards) * TILE + rank
    vmem = pl.BlockSpec(memory_space=pltpu.VMEM)
    return pl.pallas_call(
        functools.partial(term_kernel, 1.0 / replicas),
        out_shape=(
            pltpu.HBM((shards, depth, 128), BF16),
            pltpu.HBM((2, rows, rank), F32),
        ),
        in_specs=[vmem] * 3,
        out_specs=(vmem, vmem),
        compiler_params=pltpu.CompilerParams(vmem_limit_bytes=16 << 20),
    )(*in_vmem(arrived, query_full, output_full))


def finish_kernel(replica, arrived, rows, query_weight, output_weight, *refs):
    fulls, errors_out = refs[:2], refs[2:4]
    weights_out, (cols, errors, sent, weights, given) = refs[4:6], refs[6:]
    priors = [
        pltpu.make_async_copy(w, weights.at[i], given.at[i])
        for i, w in enumerate((query_weight, output_weight))
    ]
    for prior in priors:
        prior.start()
    chunks = 4
    full_width = cols.shape[1]
    width = full_width // chunks
    here = [pl.ds(c * width, width) for c in range(chunks)]

    def result(i, c):
        return pltpu.make_async_copy(
            errors.at[i, :, here[c]], errors_out[i].at[0, :, here[c]], sent.at[i, c]
        )

    each = [(i, c) for i in range(2) for c in range(chunks)]
    blocks = full_width // 128
    groups = cols.shape[0] // TILE
    per_shard = arrived.shape[1] // TILE
    for g in range(groups):
        for b in range(blocks):
            s, at = tile_of(g, b, blocks, per_shard)
            cols[g * TILE : (g + 1) * TILE, b * 128 : (b + 1) * 128] = arrived[s, at : at + TILE, :]
    rank = cols.shape[0] // 2
    for i, c in each:
        right = cols[i * rank : (i + 1) * rank, here[c]]
        approx = contract(rows[i], jnp.concatenate([right, right], axis=0), (1, 0))
        errors[i, :, here[c]] = (fulls[i][:, here[c]] - approx).astype(BF16)
        result(i, c).start()
    span = query_weight.shape[1]
    window = 384
    at = replica[0] * span
    base = jnp.minimum(at // 128 * 128, full_width - window)
    own = cols[:, pl.ds(pl.multiple_of(base, 128), window)].astype(F32)
    own = pltpu.roll(own, window - (at - base), 1)[:, :span].astype(BF16)
    for i in range(2):
        right = own[i * rank : (i + 1) * rank]
        approx = contract(rows[i], jnp.concatenate([right, right], axis=0), (1, 0))
        priors[i].wait()
        weights_out[i][...] = weights[i] - approx
    for i, c in each:
        result(i, c).wait()


def finish(arrived, rows, fulls, weights, replica):
    height, width = fulls[0].shape
    rank = rows.shape[-1] // 2
    vmem = pl.BlockSpec(memory_space=pltpu.VMEM)
    anywhere = pl.BlockSpec(memory_space=pl.ANY)
    return pl.pallas_call(
        finish_kernel,
        out_shape=(
            *[jax.ShapeDtypeStruct((1, height, width), BF16)] * 2,
            *[jax.ShapeDtypeStruct(weights[0].shape, F32)] * 2,
        ),
        in_specs=[
            pl.BlockSpec(memory_space=pltpu.SMEM),
            vmem,
            vmem,
            *[pl.BlockSpec(memory_space=pltpu.HBM)] * 2,
            vmem,
            vmem,
        ],
        out_specs=(anywhere, anywhere, vmem, vmem),
        scratch_shapes=[
            pltpu.VMEM((2 * rank, width), BF16),
            pltpu.VMEM((2, height, width), BF16),
            pltpu.SemaphoreType.DMA((2, 4)),
            pltpu.VMEM((2, *weights[0].shape), F32),
            pltpu.SemaphoreType.DMA((2,)),
        ],
        compiler_params=pltpu.CompilerParams(vmem_limit_bytes=16 << 20),
    )(replica, arrived, *in_vmem(rows), *in_hbm(*weights), *in_vmem(*fulls))


def contract(a, b, dims):
    return lax.dot_general(a, b, ((dims[:1], dims[1:]), ((), ())), preferred_element_type=F32)


def step(
    hidden_in,
    context_in,
    query_cotan,
    output_cotan,
    query_error,
    output_error,
    query_weight,
    output_weight,
    start_factors,
):
    replicas = lax.axis_size("dp")
    shards = lax.axis_size("shard")
    shard = lax.axis_index("shard").reshape(1)
    replica = lax.axis_index("dp").reshape(1)
    query_mine = (by_exchange(query_cotan),)
    output_mine = by_rings(output_cotan)
    column, right, far_low, far_high, left = output_mine
    column = partner(column)
    right, left = partner(right), partner(left)
    far_low, far_high = partner(far_low), partner(far_high)
    query_theirs = [partner(a) for a in query_mine]
    rows, rank = output_error.shape[1], start_factors.shape[-1]
    output_full, output_left = full_gradient(
        context_in,
        output_error,
        start_factors,
        1,
        (*output_mine, column, right, far_low, far_high, left),
        shard,
        pltpu.VMEM((rows, rank), F32),
    )
    query_full, lefts = full_gradient(
        hidden_in,
        query_error,
        start_factors,
        0,
        (*query_mine, *query_theirs),
        shard,
        pltpu.VMEM((replicas, rows // 2, 4 * rank), BF16),
        output_left,
    )

    sent, lefts = terms(exchange(lefts, "dp"), query_full, output_full, replicas, shards)
    depth = sent.shape[1] - rank
    shares, grams = summed(exchange(sent, "shard"), replicas, depth, 1.0)
    shares = exchange(shares, "dp")
    weighted = weighted_lefts(grams, lefts)
    (cols,) = summed(shares, shards, depth, 1.0 / replicas)
    cols = exchange(cols, "shard")
    return finish(
        cols,
        weighted,
        (query_full, output_full),
        (query_weight, output_weight),
        replica,
    )


def solution(mesh):
    placed = (
        P("dp", "shard"),
        P("dp", "shard"),
        P("dp", "shard"),
        P("dp", "shard"),
        P("dp", "shard", None),
        P("dp", "shard", None),
        P("shard", "dp"),
        P("shard", "dp"),
        P(),
    )
    return jax.shard_map(
        step,
        mesh=mesh,
        in_specs=placed,
        out_specs=(
            P("dp", "shard", None),
            P("dp", "shard", None),
            P("shard", "dp"),
            P("shard", "dp"),
        ),
        check_vma=False,
    )
```

```python
import functools

import jax
import jax.numpy as jnp
from jax import lax
from jax.experimental import pallas as pl
from jax.experimental.pallas import tpu as pltpu
from jax.sharding import PartitionSpec as P


HIGH = lax.Precision.HIGHEST
F32 = jnp.float32
BF16 = jnp.bfloat16


def copies(array, count):
    return jnp.broadcast_to(array, (count, *array.shape))


def exchange(array, axis, groups=None):
    return lax.all_to_all(array, axis, 0, 0, tiled=True, axis_index_groups=groups)


def split_high_low(array):
    high = array.astype(BF16)
    return high, (array - high.astype(F32)).astype(BF16)


def in_plane(rows, cols, core):
    side = 4
    pairs = []
    for y in range(side):
        for x in range(side):
            for c in range(2):
                to = ((y + rows) % side * side + (x + cols) % side) * 2 + (c + core) % 2
                pairs.append(((y * side + x) * 2 + c, to))
    return pairs


def send(array, rows, cols, core=0):
    return lax.ppermute(array, "shard", in_plane(rows, cols, core))


def by_exchange(cotan):
    side = 4
    rows = [[(y * side + x) * 2 + c for x in range(side)] for y in range(side) for c in range(2)]
    cols = [[(y * side + x) * 2 + c for y in range(side)] for x in range(side) for c in range(2)]
    row = exchange(copies(cotan.T, side), "shard", rows)
    return exchange(copies(row, side), "shard", cols)


def by_rings(cotan):
    block = cotan.T
    below, above, across = send(block, 1, 0), send(block, 3, 0), send(block, 2, 0)
    column = jnp.stack([block, above, across, below])
    left, right = send(column, 0, 1), send(column, 0, 3)
    half = column.shape[0] // 2
    far_low, far_high = send(left[:half], 0, 1), send(right[half:], 0, 3)
    return column, right, far_low, far_high, left


def partner(array):
    return send(array, 0, 0, 1)


def gradient_kernel(shard, *refs):
    output, query, (start_in, query_full, output_full, lefts) = refs[:12], refs[12:16], refs[16:20]
    acts, error, start, columns, given, near, done = refs[20:]
    side, each = 4, columns.shape[2] // 8
    y0, x0, core = shard[0] // 8, shard[0] // 2 % side, shard[0] % 2
    jobs = [(output, output_full, 1, True), (query, query_full, 0, False)]

    def block(refs, j, k):
        if len(refs) == 1:
            return refs[0].at[j, k]
        near, right, far_low, far_high, left = refs
        if k == 2:
            return (far_low if j < 2 else far_high).at[j % 2]
        return (near, right, None, left)[k].at[j]

    def fetch(refs, job, in_rings, j, k, other):
        x = (x0 + k) % side if in_rings else k
        at = (x * 2 + (1 - core if other else core)) * each
        count = (len(refs) - 2) // 2
        return pltpu.make_async_copy(
            block(refs[2 + count :] if other else refs[2 : 2 + count], j, k),
            columns.at[job, j, pl.ds(pl.multiple_of(at, 16), each), :],
            done.at[job, j, k * 2 + other],
        )

    def lanes(in_rings, j):
        y = (y0 + j) % side if in_rings else j
        return pl.ds(pl.multiple_of(y * (8 * each), 128), 8 * each)

    def prior(refs, job, in_rings, j):
        here = lanes(in_rings, j)
        return pltpu.make_async_copy(refs[1].at[:, here], error.at[job, j], near.at[job, j])

    steps = [(k, other) for k in range(side) for other in range(2)]
    first = pltpu.make_async_copy(start_in, start, given.at[2])
    for job, (refs, _, _, in_rings) in enumerate(jobs):
        pltpu.make_async_copy(refs[0], acts.at[job], given.at[job]).start()
        for j in range(side):
            for k, other in steps:
                fetch(refs, job, in_rings, j, k, other).start()
            prior(refs, job, in_rings, j).start()
            if job == 0 and j == 0:
                first.start()
    totals = []
    for job, (refs, full, factor, in_rings) in enumerate(jobs):
        pltpu.make_async_copy(refs[0], acts.at[job], given.at[job]).wait()
        total = jnp.zeros((acts.shape[1], start.shape[1]), F32)
        for j in range(side):
            for k, other in steps:
                fetch(refs, job, in_rings, j, k, other).wait()
            prior(refs, job, in_rings, j).wait()
            if job == 0 and j == 0:
                first.wait()
            part = contract(acts[job], columns[job, j], (1, 1)) + error[job, j].astype(F32)
            here = lanes(in_rings, j)
            full[:, here] = part
            high, low = split_high_low(part)
            rows = start[factor, :, here]
            total += contract(high, rows, (1, 1)) + contract(low, rows, (1, 1))
        totals.append(total)
    half = acts.shape[1] // 2
    packed = jnp.concatenate(
        [totals[1][:half], totals[0][:half], totals[1][half:], totals[0][half:]], axis=1
    ).astype(BF16)
    for r in range(lefts.shape[0]):
        lefts[r] = packed


def in_vmem(*arrays):
    return [pltpu.with_memory_space_constraint(a, pltpu.VMEM) for a in arrays]


def in_hbm(*arrays):
    return [pltpu.with_memory_space_constraint(a, pltpu.HBM) for a in arrays]


def full_gradients(output, query, factors, shard, replicas):
    rows, tokens = query[0].shape[::-1]
    width, rank = query[1].shape[-1], factors.shape[-1]
    vmem = pl.BlockSpec(memory_space=pltpu.VMEM)
    given = [
        a for inputs, error, *blocks in (output, query) for a in (inputs.T, error[0], *blocks)
    ]
    given.append(jnp.swapaxes(factors, 1, 2))
    return pl.pallas_call(
        gradient_kernel,
        out_shape=(
            pltpu.VMEM((rows, width), F32),
            pltpu.VMEM((rows, width), F32),
            pltpu.VMEM((replicas, rows // 2, 4 * rank), BF16),
        ),
        in_specs=[
            pl.BlockSpec(memory_space=pltpu.SMEM),
            *[pl.BlockSpec(memory_space=pltpu.HBM)] * len(given),
        ],
        out_specs=(vmem, vmem, vmem),
        scratch_shapes=[
            pltpu.VMEM((2, rows, tokens), BF16),
            pltpu.VMEM((2, 4, rows, width // 4), BF16),
            pltpu.VMEM((2, rank, width), BF16),
            pltpu.VMEM((2, 4, width // 4, tokens), BF16),
            pltpu.SemaphoreType.DMA((3,)),
            pltpu.SemaphoreType.DMA((2, 4)),
            pltpu.SemaphoreType.DMA((2, 4, 8)),
        ],
        compiler_params=pltpu.CompilerParams(vmem_limit_bytes=28 << 20),
    )(shard, *in_hbm(*given))


def inverse_kernel(grams, lefts, rows):
    rank = grams.shape[0]
    lane = lax.broadcasted_iota(jnp.int32, (rank, 4 * rank), 1)
    row = lax.broadcasted_iota(jnp.int32, (rank, 4 * rank), 0)
    given = grams[...]
    unit = (row[:, :rank] == lane[:, :rank]).astype(F32)
    state = jnp.concatenate(
        [
            given[:, :rank] + given[:, rank : 2 * rank],
            unit,
            given[:, 2 * rank : 3 * rank] + given[:, 3 * rank :],
            unit,
        ],
        axis=1,
    )
    query = lane < 2 * rank
    for k in range(rank):
        column = jnp.where(
            query, state[:, k : k + 1], state[:, 2 * rank + k : 2 * rank + k + 1]
        )
        pivot = state[k : k + 1, :] / column[k : k + 1, :]
        state = jnp.where(row == k, pivot, state - column * pivot)
    for i in range(2):
        inverse = state[:, (2 * i + 1) * rank : (2 * i + 2) * rank]
        product = jnp.dot(lefts[i], inverse, precision=HIGH, preferred_element_type=F32)
        rows[i] = jnp.concatenate(split_high_low(product), axis=1)


def weighted_lefts(grams, lefts):
    vmem = pl.BlockSpec(memory_space=pltpu.VMEM)
    return pl.pallas_call(
        inverse_kernel,
        out_shape=pltpu.VMEM((*lefts.shape[:2], 2 * lefts.shape[2]), BF16),
        in_specs=[vmem, vmem],
        out_specs=vmem,
        compiler_params=pltpu.CompilerParams(vmem_limit_bytes=8 << 20),
    )(grams, lefts)


TILE = 16


def tile_of(group, block, blocks, per_shard):
    at = group * blocks + block
    return at // per_shard, at % per_shard * TILE


def sum_kernel(scale, arrived, copies_out, *rest):
    total = arrived[0].astype(F32)
    for r in range(1, arrived.shape[0]):
        total += arrived[r].astype(F32)
    depth = copies_out.shape[1]
    share = (total[:depth] * scale).astype(BF16)
    for r in range(copies_out.shape[0]):
        copies_out[r] = share
    for kept in rest:
        kept[...] = total[depth:]


def summed(arrived, receivers, depth, scale):
    vmem = pl.BlockSpec(memory_space=pltpu.VMEM)
    kept = arrived.shape[1] - depth
    out = [pltpu.HBM((receivers, depth, 128), BF16)]
    if kept:
        out.append(pltpu.HBM((kept, 128), F32))
    return pl.pallas_call(
        functools.partial(sum_kernel, scale),
        out_shape=out,
        in_specs=[vmem],
        out_specs=[vmem] * len(out),
        compiler_params=pltpu.CompilerParams(vmem_limit_bytes=8 << 20),
    )(arrived)


def term_kernel(scale, arrived, *refs):
    *fulls, sent, left_out = refs
    total = arrived[0].astype(F32)
    for r in range(1, arrived.shape[0]):
        total += arrived[r].astype(F32)
    total = total * scale
    rank = total.shape[1] // 4
    lefts = [
        jnp.concatenate(
            [total[:, i * rank : (i + 1) * rank], total[:, (i + 2) * rank : (i + 3) * rank]], axis=0
        )
        for i in range(2)
    ]
    left_out[0] = lefts[0]
    left_out[1] = lefts[1]
    shards, depth = sent.shape[:2]
    share = depth - rank
    grams = []
    for left in lefts:
        gram = lax.dot_general(
            left, left, (((0,), (0,)), ((), ())), precision=HIGH, preferred_element_type=F32
        )
        grams.extend(split_high_low(gram))
    grams = jnp.concatenate(grams, axis=1)
    for s in range(shards):
        sent[s, share:, :] = grams
    full_width = fulls[0].shape[1]
    blocks = full_width // 128
    per_shard = share // TILE
    for t in range(2 * rank // TILE * blocks, shards * per_shard):
        sent[t // per_shard, t % per_shard * TILE : (t % per_shard + 1) * TILE, :] = jnp.zeros(
            (TILE, 128), BF16
        )
    for i in range(2):
        high, low = split_high_low(lefts[i].T)
        both = jnp.concatenate([high, low], axis=0)
        for c in range(4):
            width = full_width // 4
            full_high, full_low = split_high_low(fulls[i][:, c * width : (c + 1) * width])
            product = contract(both, full_high, (1, 0))
            product = product[:rank] + product[rank:] + contract(high, full_low, (1, 0))
            product = product.astype(BF16)
            for g in range(rank // TILE):
                for b in range(width // 128):
                    s, at = tile_of(
                        i * (rank // TILE) + g, c * (width // 128) + b, blocks, per_shard
                    )
                    sent[s, at : at + TILE, :] = product[
                        g * TILE : (g + 1) * TILE, b * 128 : (b + 1) * 128
                    ]


def terms(arrived, query_full, output_full, replicas, shards):
    rows, width = query_full.shape
    rank = arrived.shape[-1] // 4
    tiles = 2 * rank // TILE * (width // 128)
    depth = -(-tiles // shards) * TILE + rank
    vmem = pl.BlockSpec(memory_space=pltpu.VMEM)
    return pl.pallas_call(
        functools.partial(term_kernel, 1.0 / replicas),
        out_shape=(
            pltpu.HBM((shards, depth, 128), BF16),
            pltpu.HBM((2, rows, rank), F32),
        ),
        in_specs=[vmem] * 3,
        out_specs=(vmem, vmem),
        compiler_params=pltpu.CompilerParams(vmem_limit_bytes=16 << 20),
    )(*in_vmem(arrived, query_full, output_full))


def finish_kernel(replica, arrived, rows, query_weight, output_weight, *refs):
    fulls, errors_out = refs[:2], refs[2:4]
    weights_out, (cols, errors, sent, weights, given) = refs[4:6], refs[6:]
    priors = [
        pltpu.make_async_copy(w, weights.at[i], given.at[i])
        for i, w in enumerate((query_weight, output_weight))
    ]
    for prior in priors:
        prior.start()
    chunks = 4
    full_width = cols.shape[1]
    width = full_width // chunks
    here = [pl.ds(c * width, width) for c in range(chunks)]

    def result(i, c):
        return pltpu.make_async_copy(
            errors.at[i, :, here[c]], errors_out[i].at[0, :, here[c]], sent.at[i, c]
        )

    each = [(i, c) for i in range(2) for c in range(chunks)]
    blocks = full_width // 128
    groups = cols.shape[0] // TILE
    per_shard = arrived.shape[1] // TILE
    for g in range(groups):
        for b in range(blocks):
            s, at = tile_of(g, b, blocks, per_shard)
            cols[g * TILE : (g + 1) * TILE, b * 128 : (b + 1) * 128] = arrived[s, at : at + TILE, :]
    rank = cols.shape[0] // 2
    for i, c in each:
        right = cols[i * rank : (i + 1) * rank, here[c]]
        approx = contract(rows[i], jnp.concatenate([right, right], axis=0), (1, 0))
        errors[i, :, here[c]] = (fulls[i][:, here[c]] - approx).astype(BF16)
        result(i, c).start()
    span = query_weight.shape[1]
    window = 384
    at = replica[0] * span
    base = jnp.minimum(at // 128 * 128, full_width - window)
    own = cols[:, pl.ds(pl.multiple_of(base, 128), window)].astype(F32)
    own = pltpu.roll(own, window - (at - base), 1)[:, :span].astype(BF16)
    for i in range(2):
        right = own[i * rank : (i + 1) * rank]
        approx = contract(rows[i], jnp.concatenate([right, right], axis=0), (1, 0))
        priors[i].wait()
        weights_out[i][...] = weights[i] - approx
    for i, c in each:
        result(i, c).wait()


def finish(arrived, rows, fulls, weights, replica):
    height, width = fulls[0].shape
    rank = rows.shape[-1] // 2
    vmem = pl.BlockSpec(memory_space=pltpu.VMEM)
    anywhere = pl.BlockSpec(memory_space=pl.ANY)
    return pl.pallas_call(
        finish_kernel,
        out_shape=(
            *[jax.ShapeDtypeStruct((1, height, width), BF16)] * 2,
            *[jax.ShapeDtypeStruct(weights[0].shape, F32)] * 2,
        ),
        in_specs=[
            pl.BlockSpec(memory_space=pltpu.SMEM),
            vmem,
            vmem,
            *[pl.BlockSpec(memory_space=pltpu.HBM)] * 2,
            vmem,
            vmem,
        ],
        out_specs=(anywhere, anywhere, vmem, vmem),
        scratch_shapes=[
            pltpu.VMEM((2 * rank, width), BF16),
            pltpu.VMEM((2, height, width), BF16),
            pltpu.SemaphoreType.DMA((2, 4)),
            pltpu.VMEM((2, *weights[0].shape), F32),
            pltpu.SemaphoreType.DMA((2,)),
        ],
        compiler_params=pltpu.CompilerParams(vmem_limit_bytes=16 << 20),
    )(replica, arrived, *in_vmem(rows), *in_hbm(*weights), *in_vmem(*fulls))


def contract(a, b, dims):
    return lax.dot_general(a, b, ((dims[:1], dims[1:]), ((), ())), preferred_element_type=F32)


def step(
    hidden_in,
    context_in,
    query_cotan,
    output_cotan,
    query_error,
    output_error,
    query_weight,
    output_weight,
    start_factors,
):
    replicas = lax.axis_size("dp")
    shards = lax.axis_size("shard")
    shard = lax.axis_index("shard").reshape(1)
    replica = lax.axis_index("dp").reshape(1)
    query_mine = (by_exchange(query_cotan),)
    output_mine = by_rings(output_cotan)
    column, right, far_low, far_high, left = output_mine
    column = partner(column)
    right, left = partner(right), partner(left)
    far_low, far_high = partner(far_low), partner(far_high)
    query_theirs = [partner(a) for a in query_mine]
    rank = start_factors.shape[-1]
    query_full, output_full, lefts = full_gradients(
        (context_in, output_error, *output_mine, column, right, far_low, far_high, left),
        (hidden_in, query_error, *query_mine, *query_theirs),
        start_factors,
        shard,
        replicas,
    )

    sent, lefts = terms(exchange(lefts, "dp"), query_full, output_full, replicas, shards)
    depth = sent.shape[1] - rank
    shares, grams = summed(exchange(sent, "shard"), replicas, depth, 1.0)
    shares = exchange(shares, "dp")
    weighted = weighted_lefts(grams, lefts)
    (cols,) = summed(shares, shards, depth, 1.0 / replicas)
    cols = exchange(cols, "shard")
    return finish(
        cols,
        weighted,
        (query_full, output_full),
        (query_weight, output_weight),
        replica,
    )


def solution(mesh):
    placed = (
        P("dp", "shard"),
        P("dp", "shard"),
        P("dp", "shard"),
        P("dp", "shard"),
        P("dp", "shard", None),
        P("dp", "shard", None),
        P("shard", "dp"),
        P("shard", "dp"),
        P(),
    )
    return jax.shard_map(
        step,
        mesh=mesh,
        in_specs=placed,
        out_specs=(
            P("dp", "shard", None),
            P("dp", "shard", None),
            P("shard", "dp"),
            P("shard", "dp"),
        ),
        check_vma=False,
    )
```

```python
import functools

import jax
import jax.numpy as jnp
from jax import lax
from jax.experimental import pallas as pl
from jax.experimental.pallas import tpu as pltpu
from jax.sharding import PartitionSpec as P


HIGH = lax.Precision.HIGHEST
F32 = jnp.float32
BF16 = jnp.bfloat16


def copies(array, count):
    return jnp.broadcast_to(array, (count, *array.shape))


def exchange(array, axis, groups=None):
    return lax.all_to_all(array, axis, 0, 0, tiled=True, axis_index_groups=groups)


def split_high_low(array):
    high = array.astype(BF16)
    return high, (array - high.astype(F32)).astype(BF16)


def in_plane(rows, cols, core):
    side = 4
    pairs = []
    for y in range(side):
        for x in range(side):
            for c in range(2):
                to = ((y + rows) % side * side + (x + cols) % side) * 2 + (c + core) % 2
                pairs.append(((y * side + x) * 2 + c, to))
    return pairs


def send(array, rows, cols, core=0):
    return lax.ppermute(array, "shard", in_plane(rows, cols, core))


def by_exchange(cotan):
    side = 4
    rows = [[(y * side + x) * 2 + c for x in range(side)] for y in range(side) for c in range(2)]
    cols = [[(y * side + x) * 2 + c for y in range(side)] for x in range(side) for c in range(2)]
    row = exchange(copies(cotan.T, side), "shard", rows)
    return exchange(copies(row, side), "shard", cols)


def by_rings(cotan):
    block = cotan.T
    below, above, across = send(block, 1, 0), send(block, 3, 0), send(block, 2, 0)
    column = jnp.stack([block, above, across, below])
    left, right = send(column, 0, 1), send(column, 0, 3)
    half = column.shape[0] // 2
    far_low, far_high = send(left[:half], 0, 1), send(right[half:], 0, 3)
    return column, right, far_low, far_high, left


def partner(array):
    return send(array, 0, 0, 1)


def gradient_kernel(factor, shard, *refs):
    acts_in, error_in, start_in, *sources = refs[:-9]
    full, left, acts, error, start, columns, given, near, done = refs[-9:]
    in_rings = len(sources) > 3
    other_left = None if in_rings else sources.pop()
    mine, theirs = sources[: len(sources) // 2], sources[len(sources) // 2 :]
    side, each = 4, columns.shape[1] // 8
    y0, x0, core = shard[0] // 8, shard[0] // 2 % side, shard[0] % 2

    def block(refs, j, k):
        if not in_rings:
            return refs[0].at[j, k]
        near, right, far_low, far_high, left = refs
        if k == 2:
            return (far_low if j < 2 else far_high).at[j % 2]
        return (near, right, None, left)[k].at[j]

    def fetch(j, k, other):
        x = (x0 + k) % side if in_rings else k
        at = (x * 2 + (1 - core if other else core)) * each
        return pltpu.make_async_copy(
            block(theirs if other else mine, j, k),
            columns.at[j, pl.ds(pl.multiple_of(at, 16), each), :],
            done.at[j, k * 2 + other],
        )

    def lanes(j):
        y = (y0 + j) % side if in_rings else j
        return pl.ds(pl.multiple_of(y * (8 * each), 128), 8 * each)

    def prior(j):
        return pltpu.make_async_copy(error_in.at[:, lanes(j)], error.at[j], near.at[j])

    first = pltpu.make_async_copy(acts_in, acts, given.at[0])
    second = pltpu.make_async_copy(start_in.at[factor], start, given.at[1])
    first.start()
    steps = [(k, other) for k in range(side) for other in range(2)]

    def begin(j):
        for k, other in steps:
            fetch(j, k, other).start()
        prior(j).start()

    begin(0)
    second.start()
    begin(1)
    first.wait()
    total = jnp.zeros((acts.shape[0], start.shape[0]), F32)
    for j in range(side):
        for k, other in steps:
            fetch(j, k, other).wait()
        prior(j).wait()
        if j == 0:
            second.wait()
        if j + 2 < side:
            begin(j + 2)
        part = contract(acts[...], columns[j], (1, 1)) + error[j].astype(F32)
        full[:, lanes(j)] = part
        high, low = split_high_low(part)
        rows = start[:, lanes(j)]
        total += contract(high, rows, (1, 1)) + contract(low, rows, (1, 1))
    if in_rings:
        left[...] = total
    else:
        half = total.shape[0] // 2
        packed = jnp.concatenate(
            [total[:half], other_left[:half], total[half:], other_left[half:]], axis=1
        ).astype(BF16)
        for r in range(left.shape[0]):
            left[r] = packed


def in_vmem(*arrays):
    return [pltpu.with_memory_space_constraint(a, pltpu.VMEM) for a in arrays]


def in_hbm(*arrays):
    return [pltpu.with_memory_space_constraint(a, pltpu.HBM) for a in arrays]


def full_gradient(inputs, error, factors, factor, blocks, shard, left, *lefts):
    rows, tokens = inputs.shape[::-1]
    width = error.shape[-1]
    vmem = pl.BlockSpec(memory_space=pltpu.VMEM)
    return pl.pallas_call(
        functools.partial(gradient_kernel, factor),
        out_shape=(pltpu.VMEM((rows, width), F32), left),
        in_specs=[
            pl.BlockSpec(memory_space=pltpu.SMEM),
            *[pl.BlockSpec(memory_space=pltpu.HBM)] * 3,
            *[pl.BlockSpec(memory_space=pltpu.HBM)] * len(blocks),
            *[vmem] * len(lefts),
        ],
        out_specs=(vmem, vmem),
        scratch_shapes=[
            pltpu.VMEM((rows, tokens), BF16),
            pltpu.VMEM((4, rows, width // 4), BF16),
            pltpu.VMEM((factors.shape[-1], width), BF16),
            pltpu.VMEM((4, width // 4, tokens), BF16),
            pltpu.SemaphoreType.DMA((2,)),
            pltpu.SemaphoreType.DMA((4,)),
            pltpu.SemaphoreType.DMA((4, 8)),
        ],
        compiler_params=pltpu.CompilerParams(vmem_limit_bytes=20 << 20),
    )(shard, *in_hbm(inputs.T, error[0], jnp.swapaxes(factors, 1, 2), *blocks), *in_vmem(*lefts))


def inverse_kernel(grams, lefts, rows):
    rank = grams.shape[0]
    lane = lax.broadcasted_iota(jnp.int32, (rank, 4 * rank), 1)
    row = lax.broadcasted_iota(jnp.int32, (rank, 4 * rank), 0)
    given = grams[...]
    unit = (row[:, :rank] == lane[:, :rank]).astype(F32)
    state = jnp.concatenate(
        [
            given[:, :rank] + given[:, rank : 2 * rank],
            unit,
            given[:, 2 * rank : 3 * rank] + given[:, 3 * rank :],
            unit,
        ],
        axis=1,
    )
    query = lane < 2 * rank
    for k in range(rank):
        column = jnp.where(
            query, state[:, k : k + 1], state[:, 2 * rank + k : 2 * rank + k + 1]
        )
        pivot = state[k : k + 1, :] / column[k : k + 1, :]
        state = jnp.where(row == k, pivot, state - column * pivot)
    for i in range(2):
        inverse = state[:, (2 * i + 1) * rank : (2 * i + 2) * rank]
        product = jnp.dot(lefts[i], inverse, precision=HIGH, preferred_element_type=F32)
        rows[i] = jnp.concatenate(split_high_low(product), axis=1)


def weighted_lefts(grams, lefts):
    vmem = pl.BlockSpec(memory_space=pltpu.VMEM)
    return pl.pallas_call(
        inverse_kernel,
        out_shape=pltpu.VMEM((*lefts.shape[:2], 2 * lefts.shape[2]), BF16),
        in_specs=[vmem, vmem],
        out_specs=vmem,
        compiler_params=pltpu.CompilerParams(vmem_limit_bytes=8 << 20),
    )(grams, lefts)


TILE = 16


def tile_of(group, block, blocks, per_shard):
    at = group * blocks + block
    return at // per_shard, at % per_shard * TILE


def sum_kernel(scale, arrived, copies_out, *rest):
    total = arrived[0].astype(F32)
    for r in range(1, arrived.shape[0]):
        total += arrived[r].astype(F32)
    depth = copies_out.shape[1]
    share = (total[:depth] * scale).astype(BF16)
    for r in range(copies_out.shape[0]):
        copies_out[r] = share
    for kept in rest:
        kept[...] = total[depth:]


def summed(arrived, receivers, depth, scale):
    vmem = pl.BlockSpec(memory_space=pltpu.VMEM)
    kept = arrived.shape[1] - depth
    out = [pltpu.HBM((receivers, depth, 128), BF16)]
    if kept:
        out.append(pltpu.HBM((kept, 128), F32))
    return pl.pallas_call(
        functools.partial(sum_kernel, scale),
        out_shape=out,
        in_specs=[vmem],
        out_specs=[vmem] * len(out),
        compiler_params=pltpu.CompilerParams(vmem_limit_bytes=8 << 20),
    )(arrived)


def term_kernel(scale, arrived, *refs):
    *fulls, sent, left_out = refs
    total = arrived[0].astype(F32)
    for r in range(1, arrived.shape[0]):
        total += arrived[r].astype(F32)
    total = total * scale
    rank = total.shape[1] // 4
    lefts = [
        jnp.concatenate(
            [total[:, i * rank : (i + 1) * rank], total[:, (i + 2) * rank : (i + 3) * rank]], axis=0
        )
        for i in range(2)
    ]
    left_out[0] = lefts[0]
    left_out[1] = lefts[1]
    shards, depth = sent.shape[:2]
    share = depth - rank
    grams = []
    for left in lefts:
        gram = lax.dot_general(
            left, left, (((0,), (0,)), ((), ())), precision=HIGH, preferred_element_type=F32
        )
        grams.extend(split_high_low(gram))
    grams = jnp.concatenate(grams, axis=1)
    for s in range(shards):
        sent[s, share:, :] = grams
    full_width = fulls[0].shape[1]
    blocks = full_width // 128
    per_shard = share // TILE
    for t in range(2 * rank // TILE * blocks, shards * per_shard):
        sent[t // per_shard, t % per_shard * TILE : (t % per_shard + 1) * TILE, :] = jnp.zeros(
            (TILE, 128), BF16
        )
    for i in range(2):
        high, low = split_high_low(lefts[i].T)
        both = jnp.concatenate([high, low], axis=0)
        for c in range(4):
            width = full_width // 4
            full_high, full_low = split_high_low(fulls[i][:, c * width : (c + 1) * width])
            product = contract(both, full_high, (1, 0))
            product = product[:rank] + product[rank:] + contract(high, full_low, (1, 0))
            product = product.astype(BF16)
            for g in range(rank // TILE):
                for b in range(width // 128):
                    s, at = tile_of(
                        i * (rank // TILE) + g, c * (width // 128) + b, blocks, per_shard
                    )
                    sent[s, at : at + TILE, :] = product[
                        g * TILE : (g + 1) * TILE, b * 128 : (b + 1) * 128
                    ]


def terms(arrived, query_full, output_full, replicas, shards):
    rows, width = query_full.shape
    rank = arrived.shape[-1] // 4
    tiles = 2 * rank // TILE * (width // 128)
    depth = -(-tiles // shards) * TILE + rank
    vmem = pl.BlockSpec(memory_space=pltpu.VMEM)
    return pl.pallas_call(
        functools.partial(term_kernel, 1.0 / replicas),
        out_shape=(
            pltpu.HBM((shards, depth, 128), BF16),
            pltpu.HBM((2, rows, rank), F32),
        ),
        in_specs=[vmem] * 3,
        out_specs=(vmem, vmem),
        compiler_params=pltpu.CompilerParams(vmem_limit_bytes=16 << 20),
    )(*in_vmem(arrived, query_full, output_full))


def finish_kernel(replica, arrived, rows, query_weight, output_weight, *refs):
    fulls, errors_out = refs[:2], refs[2:4]
    weights_out, (cols, errors, sent, weights, given) = refs[4:6], refs[6:]
    priors = [
        pltpu.make_async_copy(w, weights.at[i], given.at[i])
        for i, w in enumerate((query_weight, output_weight))
    ]
    for prior in priors:
        prior.start()
    chunks = 4
    full_width = cols.shape[1]
    width = full_width // chunks
    here = [pl.ds(c * width, width) for c in range(chunks)]

    def result(i, c):
        return pltpu.make_async_copy(
            errors.at[i, :, here[c]], errors_out[i].at[0, :, here[c]], sent.at[i, c]
        )

    each = [(i, c) for i in range(2) for c in range(chunks)]
    blocks = full_width // 128
    groups = cols.shape[0] // TILE
    per_shard = arrived.shape[1] // TILE
    for g in range(groups):
        for b in range(blocks):
            s, at = tile_of(g, b, blocks, per_shard)
            cols[g * TILE : (g + 1) * TILE, b * 128 : (b + 1) * 128] = arrived[s, at : at + TILE, :]
    rank = cols.shape[0] // 2
    for i, c in each:
        right = cols[i * rank : (i + 1) * rank, here[c]]
        approx = contract(rows[i], jnp.concatenate([right, right], axis=0), (1, 0))
        errors[i, :, here[c]] = (fulls[i][:, here[c]] - approx).astype(BF16)
        result(i, c).start()
    span = query_weight.shape[1]
    window = 384
    at = replica[0] * span
    base = jnp.minimum(at // 128 * 128, full_width - window)
    own = cols[:, pl.ds(pl.multiple_of(base, 128), window)].astype(F32)
    own = pltpu.roll(own, window - (at - base), 1)[:, :span].astype(BF16)
    for i in range(2):
        right = own[i * rank : (i + 1) * rank]
        approx = contract(rows[i], jnp.concatenate([right, right], axis=0), (1, 0))
        priors[i].wait()
        weights_out[i][...] = weights[i] - approx
    for i, c in each:
        result(i, c).wait()


def finish(arrived, rows, fulls, weights, replica):
    height, width = fulls[0].shape
    rank = rows.shape[-1] // 2
    vmem = pl.BlockSpec(memory_space=pltpu.VMEM)
    anywhere = pl.BlockSpec(memory_space=pl.ANY)
    return pl.pallas_call(
        finish_kernel,
        out_shape=(
            *[jax.ShapeDtypeStruct((1, height, width), BF16)] * 2,
            *[jax.ShapeDtypeStruct(weights[0].shape, F32)] * 2,
        ),
        in_specs=[
            pl.BlockSpec(memory_space=pltpu.SMEM),
            vmem,
            vmem,
            *[pl.BlockSpec(memory_space=pltpu.HBM)] * 2,
            vmem,
            vmem,
        ],
        out_specs=(anywhere, anywhere, vmem, vmem),
        scratch_shapes=[
            pltpu.VMEM((2 * rank, width), BF16),
            pltpu.VMEM((2, height, width), BF16),
            pltpu.SemaphoreType.DMA((2, 4)),
            pltpu.VMEM((2, *weights[0].shape), F32),
            pltpu.SemaphoreType.DMA((2,)),
        ],
        compiler_params=pltpu.CompilerParams(vmem_limit_bytes=16 << 20),
    )(replica, arrived, *in_vmem(rows), *in_hbm(*weights), *in_vmem(*fulls))


def contract(a, b, dims):
    return lax.dot_general(a, b, ((dims[:1], dims[1:]), ((), ())), preferred_element_type=F32)


def step(
    hidden_in,
    context_in,
    query_cotan,
    output_cotan,
    query_error,
    output_error,
    query_weight,
    output_weight,
    start_factors,
):
    replicas = lax.axis_size("dp")
    shards = lax.axis_size("shard")
    shard = lax.axis_index("shard").reshape(1)
    replica = lax.axis_index("dp").reshape(1)
    query_mine = (by_exchange(query_cotan),)
    output_mine = by_rings(output_cotan)
    column, right, far_low, far_high, left = output_mine
    column = partner(column)
    right, left = partner(right), partner(left)
    far_low, far_high = partner(far_low), partner(far_high)
    query_theirs = [partner(a) for a in query_mine]
    rows, rank = output_error.shape[1], start_factors.shape[-1]
    output_full, output_left = full_gradient(
        context_in,
        output_error,
        start_factors,
        1,
        (*output_mine, column, right, far_low, far_high, left),
        shard,
        pltpu.VMEM((rows, rank), F32),
    )
    query_full, lefts = full_gradient(
        hidden_in,
        query_error,
        start_factors,
        0,
        (*query_mine, *query_theirs),
        shard,
        pltpu.VMEM((replicas, rows // 2, 4 * rank), BF16),
        output_left,
    )

    sent, lefts = terms(exchange(lefts, "dp"), query_full, output_full, replicas, shards)
    depth = sent.shape[1] - rank
    shares, grams = summed(exchange(sent, "shard"), replicas, depth, 1.0)
    shares = exchange(shares, "dp")
    weighted = weighted_lefts(grams, lefts)
    (cols,) = summed(shares, shards, depth, 1.0 / replicas)
    cols = exchange(cols, "shard")
    return finish(
        cols,
        weighted,
        (query_full, output_full),
        (query_weight, output_weight),
        replica,
    )


def solution(mesh):
    placed = (
        P("dp", "shard"),
        P("dp", "shard"),
        P("dp", "shard"),
        P("dp", "shard"),
        P("dp", "shard", None),
        P("dp", "shard", None),
        P("shard", "dp"),
        P("shard", "dp"),
        P(),
    )
    return jax.shard_map(
        step,
        mesh=mesh,
        in_specs=placed,
        out_specs=(
            P("dp", "shard", None),
            P("dp", "shard", None),
            P("shard", "dp"),
            P("shard", "dp"),
        ),
        check_vma=False,
    )
```
